256 devices in a mesh: pipe: 4 (over y), seq: 16 (over z, core), dp: 4 (over x).
Axes of the slice: x: 4, y: 4, z: 8, core: 2. Of those that a mesh axis runs over, the one named last changes fastest.
Arguments:
- section_inputs: bfloat16 [4, 4, 16, 16, 8, 512], P('pipe', 'dp', 'seq'), may hold values from -6 to 6
- w_spatial: bfloat16 [4, 9, 512, 512], P('pipe'), may hold values from -0.09375 to 0.09375
- w_temporal: bfloat16 [4, 3, 512, 512], P('pipe'), may hold values from -0.15625 to 0.15625
- grad_output: bfloat16 [4, 16, 16, 8, 512], P('dp', 'seq'), may hold values from -6 to 6
- frame_start: int32 [4], P('dp'), may hold values from 0 to 8
- frame_count: int32 [4], P('dp'), may hold values from 9 to 16
Outputs:
- grad_inputs: bfloat16 [4, 4, 16, 16, 8, 512], P('pipe', 'dp', 'seq')
- grad_spatial: float32 [4, 9, 512, 512], P('pipe', None, 'seq')
- grad_temporal: float32 [4, 3, 512, 512], P('pipe', None, 'seq')
The draws below stay inside these ranges and needn't reach their ends.
Inputs may be any that keep to these rules, and one draw needn't show every extreme that they name: For every clip c, frame_count[c] is greater than frame_start[c].
All inputs are finite; a program needn't handle non-finite values.
Results may differ from the reference program's by a relative error of at most 0.02.
Values may be sent and summed in bfloat16 or wider, within the bound.
No kernel may reach another device: no remote copies, remote signals or barrier semaphores. Data moves between devices by JAX's collectives and lax.ppermute only.
A program may use at most 192 MiB of HBM per device.

```python
import jax
import jax.numpy as jnp
from jax import lax

CHANNELS = 512
COLS = 8
FRAMES = 16
ROWS = 16
CLIPS = 4
N_PIPE = 4


def touch_ends(drawn, stream_key, smallest, largest):
    dims = drawn.shape
    index_at = [jax.random.randint(jax.random.fold_in(stream_key, axis), (), 0, dims[axis]) for axis in range(len(dims))]
    drawn = drawn.at[tuple(index_at)].set(smallest)
    longest = dims.index(max(dims))
    index_at[longest] = (index_at[longest] + 1) % dims[longest]
    return drawn.at[tuple(index_at)].set(largest)


def level_of(stream_key, dims, shards, smallest, top_value):
    gain, own = 1.0, jax.random.fold_in(stream_key, 6)
    for axis_at, shards_of in shards:
        draws = jnp.exp(jax.random.uniform(jax.random.fold_in(own, axis_at), (shards_of,), jnp.float32, smallest / len(shards), top_value / len(shards)))
        gain = gain * jnp.repeat(draws, dims[axis_at] // shards_of).reshape([-1 if axis == axis_at else 1 for axis in range(len(dims))])
    return gain


def scatter_about(own_key, dims, scale, bound, pieces=(), kind=jnp.bfloat16):
    loudness = level_of(own_key, dims, pieces, -0.22, 0.18) if pieces else 1.0
    result = jax.random.normal(own_key, dims, jnp.float32) * scale * loudness
    return jnp.minimum(jnp.maximum(result, -bound), bound).astype(kind)


def setup_inputs(seed: int = 0) -> dict:
    splits = jax.random.split(jax.random.key(seed), 7)
    section_inputs = scatter_about(splits[0], (N_PIPE, CLIPS, FRAMES, ROWS, COLS, CHANNELS), 1.0, 6.0, ((0, 4), (1, 4), (2, 16)))
    w_spatial = scatter_about(splits[1], (N_PIPE, 9, CHANNELS, CHANNELS), (9 * CHANNELS) ** -0.5, 0.09375, ((0, 4),))
    w_temporal = scatter_about(splits[2], (N_PIPE, 3, CHANNELS, CHANNELS), (3 * CHANNELS) ** -0.5, 0.15625, ((0, 4),))
    grad_output = scatter_about(splits[3], (CLIPS, FRAMES, ROWS, COLS, CHANNELS), 1.0, 6.0, ((0, 4), (1, 16)))
    frame_start = touch_ends(jax.random.randint(splits[4], (CLIPS,), 0, FRAMES // 2 + 1), jax.random.fold_in(splits[4], 1), 0, (FRAMES // 2 + 1) - 1).astype(jnp.int32)
    frame_count = touch_ends(jax.random.randint(splits[5], (CLIPS,), FRAMES // 2 + 1, FRAMES + 1), jax.random.fold_in(splits[5], 1), FRAMES // 2 + 1, FRAMES).astype(jnp.int32)
    return {"section_inputs": section_inputs, "w_spatial": w_spatial, "w_temporal": w_temporal, "grad_output": grad_output, "frame_start": frame_start, "frame_count": frame_count}


def patches(volume):
    height = volume.shape[1]
    breadth = volume.shape[2]
    padded = jnp.pad(volume, ((0, 0), (1, 1), (1, 1), (0, 0)))
    return jnp.concatenate([padded[:, row_off:row_off + height, col_off:col_off + breadth] for row_off in range(3) for col_off in range(3)], axis=-1)


def silu_slope(pre_act):
    sigmoid_value = jax.nn.sigmoid(pre_act)
    return sigmoid_value * (1.0 + pre_act * (1.0 - sigmoid_value))


def contract_rows(left, right):
    return lax.dot_general(left, right, (((0,), (0,)), ((), ())), preferred_element_type=jnp.float32)


def clip_backward(inputs, cotangent, spatial, temporal):
    frames = inputs.shape[0]
    channels = inputs.shape[-1]
    columns = patches(inputs).reshape(-1, 9 * channels)
    pre_act = jnp.dot(columns, spatial.reshape(9 * channels, channels), preferred_element_type=jnp.float32)
    activated = jax.nn.silu(pre_act).astype(jnp.bfloat16).reshape(inputs.shape)
    zero_frames = jnp.zeros((2,) + inputs.shape[1:], jnp.bfloat16)
    act_full = jnp.concatenate([zero_frames, activated], axis=0)
    cot_full = jnp.concatenate([cotangent, zero_frames], axis=0)
    act_taps = jnp.concatenate([act_full[2 - tap_index:2 - tap_index + frames] for tap_index in range(3)], axis=-1)
    cot_taps = jnp.concatenate([cot_full[tap_index:tap_index + frames] for tap_index in range(3)], axis=-1)
    grad_wt = contract_rows(act_taps.reshape(-1, 3 * channels), cotangent.reshape(-1, channels))
    w_back = jnp.transpose(temporal, (0, 2, 1)).reshape(3 * channels, channels)
    grad_act = jnp.dot(cot_taps.reshape(-1, 3 * channels), w_back, preferred_element_type=jnp.float32).astype(jnp.bfloat16)
    grad_pre = (grad_act.astype(jnp.float32) * silu_slope(pre_act)).astype(jnp.bfloat16)
    grad_ws = contract_rows(columns, grad_pre)
    w_flip = jnp.transpose(spatial[::-1], (0, 2, 1)).reshape(9 * channels, channels)
    spread = jnp.dot(patches(grad_pre.reshape(inputs.shape)).reshape(-1, 9 * channels), w_flip, preferred_element_type=jnp.float32)
    grad_in = (cotangent.astype(jnp.float32).reshape(-1, channels) + spread).astype(jnp.bfloat16).reshape(inputs.shape)
    return grad_in, grad_ws, grad_wt


def reference(section_inputs, w_spatial, w_temporal, grad_output, frame_start, frame_count):
    channels = grad_output.shape[-1]
    frame_ids = jnp.arange(FRAMES, dtype=jnp.int32)
    keep = (frame_ids[None, :] >= frame_start[:, None]) & (frame_ids[None, :] < frame_count[:, None])
    cotangent = jnp.where(keep[:, :, None, None, None], grad_output, jnp.zeros_like(grad_output))
    grads_in = []
    grads_ws = []
    grads_wt = []
    for section_index in range(N_PIPE - 1, -1, -1):
        spatial = w_spatial[section_index]
        temporal = w_temporal[section_index]

        def single(pair):
            return clip_backward(pair[0], pair[1], spatial, temporal)

        grad_in, grad_ws, grad_wt = lax.map(single, (section_inputs[section_index], cotangent))
        grads_in.append(grad_in)
        grads_ws.append(jnp.sum(grad_ws, axis=0).reshape(9, channels, channels))
        grads_wt.append(jnp.sum(grad_wt, axis=0).reshape(3, channels, channels))
        cotangent = grad_in
    return jnp.stack(grads_in[::-1]), jnp.stack(grads_ws[::-1]), jnp.stack(grads_wt[::-1])
```

```python
import functools

import jax
import jax.numpy as jnp
from jax import lax
from jax.experimental import pallas as pl
from jax.experimental.pallas import tpu as pltpu
from jax.sharding import PartitionSpec as P


F32 = jnp.float32
BF16 = jnp.bfloat16
ANY = pl.BlockSpec(memory_space=pl.ANY)
SMEM = pl.BlockSpec(memory_space=pltpu.SMEM)
VMEM = pl.BlockSpec(memory_space=pltpu.VMEM)

ROWS, COLS, CH = 16, 8, 512
CELLS = ROWS * COLS
FRAMES = 16
CLIPS = 4
SLICE = CH // FRAMES
TAPS = 12
WIDE = TAPS * SLICE
SUB = SLICE // CLIPS


def nn(a, b):
    return lax.dot_general(a, b, (((1,), (0,)), ((), ())), preferred_element_type=F32)


def nt(a, b):
    return lax.dot_general(a, b, (((1,), (1,)), ((), ())), preferred_element_type=F32)


def column_shifts(v):
    col = lax.broadcasted_iota(jnp.int32, v.shape, 0) % COLS
    before = jnp.where(col == 0, 0.0, pltpu.roll(v, 1, 0))
    after = jnp.where(col == COLS - 1, 0.0, pltpu.roll(v, CELLS - 1, 0))
    return {0: v, -1: before, 1: after}


def row_shift(v, step):
    zero = jnp.zeros((COLS, v.shape[1]), v.dtype)
    if step == 0:
        return v
    if step < 0:
        return jnp.concatenate([zero, v[:-COLS]], axis=0)
    return jnp.concatenate([v[COLS:], zero], axis=0)


def forward_kernel(x_ref, ws_hbm, act_ref, slope_ref, ws, sems):
    copies = [pltpu.make_async_copy(ws_hbm.at[k], ws.at[k], sems.at[k]) for k in range(9)]
    for c in copies:
        c.start()
    cols = column_shifts(x_ref[...].astype(F32))
    pre = None
    for r in range(3):
        for q in range(3):
            lhs = row_shift(cols[q - 1], r - 1).astype(BF16)
            copies[3 * r + q].wait()
            term = nn(lhs, ws[3 * r + q])
            pre = term if pre is None else pre + term
    s = jax.nn.sigmoid(pre)
    act_ref[...] = (pre * s).astype(BF16)
    slope_ref[...] = s * (1.0 + pre * (1.0 - s))


def forward(x, ws):
    return pl.pallas_call(
        forward_kernel,
        name="block_forward",
        out_shape=(
            jax.ShapeDtypeStruct((CELLS, CH), BF16),
            jax.ShapeDtypeStruct((CELLS, CH), F32),
        ),
        in_specs=[VMEM, ANY],
        out_specs=(VMEM, VMEM),
        scratch_shapes=[pltpu.VMEM((9, CH, CH), BF16), pltpu.SemaphoreType.DMA((9,))],
        compiler_params=pltpu.CompilerParams(vmem_limit_bytes=24 << 20),
        cost_estimate=pl.CostEstimate(flops=1208000000, bytes_accessed=5500000, transcendentals=65536),
    )(x, ws)


def section_kernel(count, emit, *refs):
    flag_ref = refs[0]
    own = refs[1:4]
    got = refs[4 : 4 + count]
    slope_ref, wt_hbm, ws_hbm = refs[4 + count : 7 + count]
    rest = refs[7 + count :]
    gin_ref = rest[0]
    late_ref = rest[1] if emit else None
    cot, wt, ws, csem, tsem, ssem = rest[2 if emit else 1 :]
    tcopies = [pltpu.make_async_copy(wt_hbm.at[k], wt.at[k], tsem.at[k]) for k in range(3)]
    scopies = [pltpu.make_async_copy(ws_hbm.at[k], ws.at[k], ssem.at[k]) for k in range(9)]

    def fetch(sources):
        for k in range(3):
            pltpu.make_async_copy(sources[k], cot.at[k], csem.at[k]).start()

    if count:
        first = flag_ref[0] == 1

        @pl.when(first)
        def _():
            fetch(own)

        @pl.when(jnp.logical_not(first))
        def _():
            fetch(got)
    else:
        fetch(own)
    for c in tcopies + scopies:
        c.start()
    grad_act = None
    for k in range(3):
        pltpu.make_async_copy(own[k], cot.at[k], csem.at[k]).wait()
        tcopies[k].wait()
        term = nt(cot[k], wt[k])
        grad_act = term if grad_act is None else grad_act + term
    grad_pre = (grad_act.astype(BF16).astype(F32) * slope_ref[...]).astype(BF16).astype(F32)
    if emit:
        late_ref[:, :SLICE] = grad_pre.T.astype(BF16).reshape(FRAMES, SLICE, CELLS)
        late_ref[:, SLICE:] = cot[0].astype(F32).T.astype(BF16).reshape(FRAMES, SLICE, CELLS)
    cols = column_shifts(grad_pre)
    total = cot[0].astype(F32)
    for r in range(3):
        for q in range(3):
            lhs = row_shift(cols[1 - q], 1 - r).astype(BF16)
            scopies[3 * r + q].wait()
            total = total + nt(lhs, ws[3 * r + q])
    gin_ref[...] = total.astype(BF16)


def section(flag, own, got, slope, wt, ws, emit):
    outs = [jax.ShapeDtypeStruct((CELLS, CH), BF16)]
    if emit:
        outs.append(jax.ShapeDtypeStruct((FRAMES, 2 * SLICE, CELLS), BF16))
    return pl.pallas_call(
        functools.partial(section_kernel, len(got), emit),
        name="section_emit" if emit else "section",
        out_shape=tuple(outs),
        in_specs=[SMEM] + [ANY] * (3 + len(got)) + [VMEM, ANY, ANY],
        out_specs=(VMEM,) * len(outs),
        scratch_shapes=[
            pltpu.VMEM((3, CELLS, CH), BF16),
            pltpu.VMEM((3, CH, CH), BF16),
            pltpu.VMEM((9, CH, CH), BF16),
            pltpu.SemaphoreType.DMA((3,)),
            pltpu.SemaphoreType.DMA((3,)),
            pltpu.SemaphoreType.DMA((9,)),
        ],
        compiler_params=pltpu.CompilerParams(vmem_limit_bytes=24 << 20),
        cost_estimate=pl.CostEstimate(flops=1600000000, bytes_accessed=7000000, transcendentals=0),
    )(flag, *own, *got, slope, wt, ws)


def weights_kernel(where_ref, late_ref, *refs):
    ring = refs[:8]
    swapped = refs[8]
    outs = refs[9:13]
    x, act, left, result, sems = refs[13:]
    z, core, d = where_ref[0], where_ref[1], where_ref[2]
    half = FRAMES // 2
    copies = []
    for k in range(half):
        chip = lax.rem(z + k, half)
        for which, source in ((core, ring[k]), (1 - core, swapped.at[k])):
            t = pl.multiple_of((2 * chip + which) * CELLS, CELLS)
            for part, target in ((0, x), (1, act)):
                n = len(copies)
                c = pltpu.make_async_copy(source.at[part], target.at[pl.ds(t, CELLS)], sems.at[n])
                c.start()
                copies.append(c)
    g = late_ref[:, :SLICE].astype(F32).reshape(FRAMES * SLICE, CELLS)
    lane = lax.broadcasted_iota(jnp.int32, g.shape, 1)
    row, col = lane // COLS, lane % COLS
    for r in range(3):
        for q in range(3):
            dr, dc = r - 1, q - 1
            v = g if dr == 0 and dc == 0 else pltpu.roll(g, (dr * COLS + dc) % CELLS, 1)
            keep = None
            for at, step, size in ((row, dr, ROWS), (col, dc, COLS)):
                if step:
                    good = (at != 0) if step > 0 else (at != size - 1)
                    keep = good if keep is None else keep & good
            if keep is not None:
                v = jnp.where(keep, v, 0.0)
            v = v.astype(BF16).reshape(FRAMES, SLICE, CELLS)
            base = (3 * r + q) * SLICE
            for f in range(FRAMES):
                left[base : base + SLICE, f * CELLS : (f + 1) * CELLS] = v[f]
    for k in range(3):
        base = (9 + k) * SLICE
        for f in range(FRAMES):
            if f + k < FRAMES:
                v = late_ref[f + k, SLICE:]
            else:
                v = jnp.zeros((SLICE, CELLS), BF16)
            left[base : base + SLICE, f * CELLS : (f + 1) * CELLS] = v
    for c in copies:
        c.wait()
    spatial = nn(left[: 9 * SLICE], x[...])
    temporal = nn(left[9 * SLICE :], act[...])
    result[:, :, :, : 9 * SLICE] = spatial.T.reshape(FRAMES, CLIPS, SUB, 9 * SLICE)
    result[:, :, :, 9 * SLICE :] = temporal.T.reshape(FRAMES, CLIPS, SUB, 3 * SLICE)
    for k in range(CLIPS):
        outs[k][...] = result[:, lax.rem(d + k, CLIPS)].astype(BF16)


def weights(where, late, ring, swapped):
    return pl.pallas_call(
        weights_kernel,
        name="weight_grads",
        out_shape=(jax.ShapeDtypeStruct((FRAMES, SUB, WIDE), BF16),) * CLIPS,
        in_specs=[SMEM, VMEM] + [ANY] * 9,
        out_specs=(VMEM,) * CLIPS,
        scratch_shapes=[
            pltpu.VMEM((FRAMES * CELLS, CH), BF16),
            pltpu.VMEM((FRAMES * CELLS, CH), BF16),
            pltpu.VMEM((WIDE, FRAMES * CELLS), BF16),
            pltpu.VMEM((FRAMES, CLIPS, SUB, WIDE), F32),
            pltpu.SemaphoreType.DMA((4 * FRAMES // 2,)),
        ],
        compiler_params=pltpu.CompilerParams(vmem_limit_bytes=24 << 20),
        cost_estimate=pl.CostEstimate(flops=1610000000, bytes_accessed=5000000, transcendentals=0),
    )(where, late, *ring, swapped)


def assemble_kernel(where_ref, *refs):
    parts, (spatial_ref, temporal_ref) = refs[:CLIPS], refs[CLIPS:]
    d = where_ref[2]
    for k in range(CLIPS):
        source = lax.rem(d + CLIPS - k, CLIPS)
        rows = pl.ds(pl.multiple_of(source * SUB, SUB), SUB)
        part = parts[k][...].astype(F32)
        for tap in range(TAPS):
            line = jnp.concatenate(
                [part[s, :, tap * SLICE : (tap + 1) * SLICE] for s in range(FRAMES)], axis=-1
            )
            if tap < 9:
                spatial_ref[tap, rows, :] = line
            else:
                temporal_ref[tap - 9, rows, :] = line


def assemble(where, parts):
    return pl.pallas_call(
        assemble_kernel,
        name="assemble",
        out_shape=(
            jax.ShapeDtypeStruct((9, SLICE, CH), F32),
            jax.ShapeDtypeStruct((3, SLICE, CH), F32),
        ),
        in_specs=[SMEM] + [VMEM] * CLIPS,
        out_specs=(VMEM, VMEM),
        compiler_params=pltpu.CompilerParams(vmem_limit_bytes=24 << 20),
        cost_estimate=pl.CostEstimate(flops=1000000, bytes_accessed=1200000, transcendentals=0),
    )(where, *parts)


def send(value, axes, sizes, step):
    pairs = []
    for a in range(sizes[0]):
        for b in range(sizes[1]):
            to = (a + step[0], b + step[1])
            if 0 <= to[0] < sizes[0] and 0 <= to[1] < sizes[1]:
                pairs.append((a * sizes[1] + b, to[0] * sizes[1] + to[1]))
    return lax.ppermute(value, axes, pairs)


def around(value, axis, size, step):
    return lax.ppermute(value, axis, [(i, (i + step) % size) for i in range(size)])


def local(sizes, section_inputs, w_spatial, w_temporal, grad_output, frame_start, frame_count):
    axes = ("pipe", "seq")
    x = section_inputs.reshape(CELLS, CH)
    ws, wt = w_spatial[0], w_temporal[0]
    seq = lax.axis_index("seq")
    where = jnp.stack([seq // 2, seq % 2, lax.axis_index("dp")]).astype(jnp.int32)
    flag = (lax.axis_index("pipe") == sizes[0] - 1).astype(jnp.int32)[None]
    keep = (seq >= frame_start[0]) & (seq < frame_count[0])
    cot = jnp.where(keep, grad_output.reshape(CELLS, CH), jnp.zeros((CELLS, CH), BF16))
    own = [cot, send(cot, axes, sizes, (0, -1)), send(cot, axes, sizes, (0, -2))]
    act, slope = forward(x, ws)
    mine = jnp.stack([x, act])
    ring = {0: mine}
    got = []
    late = None
    for step in range(sizes[0]):
        emit = step == sizes[0] - 1
        outs = section(flag, own, got, slope, wt, ws, emit)
        grad_in = outs[0]
        if emit:
            late = outs[1]
        else:
            got = [send(grad_in, axes, sizes, (-1, -k)) for k in range(3)]
        edge_up, edge_down = ring[min(ring)], ring[max(ring)]
        if not emit:
            edge_up, edge_down, _ = lax.optimization_barrier((edge_up, edge_down, grad_in))
            ring[-step - 1] = around(edge_up, "seq", FRAMES, 2)
            ring[step + 1] = around(edge_down, "seq", FRAMES, -2)
            if step == 2:
                ring[4] = around(ring[3], "seq", FRAMES, -2)
    pieces = [ring[k if k <= 4 else k - 8] for k in range(8)]
    swapped = lax.ppermute(jnp.stack(pieces), "seq", [(i, i ^ 1) for i in range(FRAMES)])
    gathered = lax.all_to_all(late, "seq", 0, 0, tiled=True)
    partial = weights(where, gathered, pieces, swapped)
    shares = [partial[0]] + [around(partial[k], "dp", CLIPS, k) for k in (1, 2, 3)]
    share = sum(s.astype(F32) for s in shares).astype(BF16)
    share = lax.all_to_all(share, "seq", 0, 0, tiled=True)
    parts = [share] + [around(share, "dp", CLIPS, k) for k in (1, 2, 3)]
    spatial, temporal = assemble(where, parts)
    return grad_in.reshape(section_inputs.shape), spatial[None], temporal[None]


def solution(mesh):
    sizes = (mesh.shape["pipe"], mesh.shape["seq"])
    placed = (
        P("pipe", "dp", "seq", None, None, None),
        P("pipe", None, None, None),
        P("pipe", None, None, None),
        P("dp", "seq", None, None, None),
        P("dp"),
        P("dp"),
    )
    return jax.shard_map(
        functools.partial(local, sizes),
        mesh=mesh,
        in_specs=placed,
        out_specs=(
            P("pipe", "dp", "seq", None, None, None),
            P("pipe", None, "seq", None),
            P("pipe", None, "seq", None),
        ),
        check_vma=False,
    )
```

```python
import functools

import jax
import jax.numpy as jnp
from jax import lax
from jax.experimental import pallas as pl
from jax.experimental.pallas import tpu as pltpu
from jax.sharding import PartitionSpec as P


F32 = jnp.float32
BF16 = jnp.bfloat16
ANY = pl.BlockSpec(memory_space=pl.ANY)
SMEM = pl.BlockSpec(memory_space=pltpu.SMEM)
VMEM = pl.BlockSpec(memory_space=pltpu.VMEM)

ROWS, COLS, CH = 16, 8, 512
CELLS = ROWS * COLS
FRAMES = 16
CLIPS = 4
SLICE = CH // FRAMES
TAPS = 12
WIDE = TAPS * SLICE
SUB = SLICE // CLIPS


def nn(a, b):
    return lax.dot_general(a, b, (((1,), (0,)), ((), ())), preferred_element_type=F32)


def nt(a, b):
    return lax.dot_general(a, b, (((1,), (1,)), ((), ())), preferred_element_type=F32)


def column_shifts(v):
    col = lax.broadcasted_iota(jnp.int32, v.shape, 0) % COLS
    before = jnp.where(col == 0, 0.0, pltpu.roll(v, 1, 0))
    after = jnp.where(col == COLS - 1, 0.0, pltpu.roll(v, CELLS - 1, 0))
    return {0: v, -1: before, 1: after}


def row_shift(v, step):
    zero = jnp.zeros((COLS, v.shape[1]), v.dtype)
    if step == 0:
        return v
    if step < 0:
        return jnp.concatenate([zero, v[:-COLS]], axis=0)
    return jnp.concatenate([v[COLS:], zero], axis=0)


def forward_kernel(x_ref, wt_ref, ws_ref, mine_ref, slope_ref, wtt_ref, wst_ref):
    x = x_ref[...].astype(F32)
    cols = column_shifts(x)
    pre = None
    for r in range(3):
        for q in range(3):
            term = nn(row_shift(cols[q - 1], r - 1).astype(BF16), ws_ref[3 * r + q])
            pre = term if pre is None else pre + term
    s = jax.nn.sigmoid(pre)
    slope_ref[...] = s * (1.0 + pre * (1.0 - s))
    mine_ref[0] = x.T.astype(BF16)
    mine_ref[1] = (pre * s).astype(BF16).astype(F32).T.astype(BF16)
    for k in range(3):
        wtt_ref[k] = wt_ref[k].T
    for k in range(9):
        wst_ref[k] = ws_ref[k].T


def forward(x, wt, ws):
    return pl.pallas_call(
        forward_kernel,
        name="block_forward",
        out_shape=(
            jax.ShapeDtypeStruct((2, CH, CELLS), BF16),
            jax.ShapeDtypeStruct((CELLS, CH), F32),
            jax.ShapeDtypeStruct((3, CH, CH), BF16),
            jax.ShapeDtypeStruct((9, CH, CH), BF16),
        ),
        in_specs=[VMEM] * 3,
        out_specs=(VMEM,) * 4,
        compiler_params=pltpu.CompilerParams(vmem_limit_bytes=24 << 20),
        cost_estimate=pl.CostEstimate(flops=1208000000, bytes_accessed=13000000, transcendentals=65536),
    )(x, wt, ws)


def cotangents(count, refs):
    start_ref, count_ref = refs[0], refs[1]
    own = refs[2:5]
    got = refs[5 : 5 + count]
    seq = lax.axis_index("seq")
    last = lax.axis_index("pipe") == lax.axis_size("pipe") - 1
    out = []
    for k in range(3):
        t = seq + k
        counted = (t >= start_ref[0]) & (t < count_ref[0])
        if count:
            value = jnp.where(last, own[k][...], got[k][...])
            keep = jnp.where(last, counted, t < FRAMES)
        else:
            value, keep = own[k][...], counted
        out.append(jnp.where(keep, value, jnp.zeros((CELLS, CH), BF16)))
    return out, refs[5 + count :]


def grad_pre_of(cot, slope_ref, wtt_ref):
    grad_act = nn(cot[0], wtt_ref[0]) + nn(cot[1], wtt_ref[1]) + nn(cot[2], wtt_ref[2])
    return (grad_act.astype(BF16).astype(F32) * slope_ref[...]).astype(BF16)


def spread_of(cot, grad_pre, wst_ref):
    cols = column_shifts(grad_pre.astype(F32))
    total = cot.astype(F32)
    for r in range(3):
        for q in range(3):
            lhs = row_shift(cols[1 - q], 1 - r).astype(BF16)
            total = total + nn(lhs, wst_ref[3 * r + q])
    return total.astype(BF16)


def section_kernel(count, *refs):
    cot, (slope_ref, wtt_ref, wst_ref, gin_ref) = cotangents(count, refs)
    grad_pre = grad_pre_of(cot, slope_ref, wtt_ref)
    gin_ref[...] = spread_of(cot[0], grad_pre, wst_ref)


def emit_kernel(count, *refs):
    cot, (slope_ref, wtt_ref, late_ref, cot_ref, pre_ref) = cotangents(count, refs)
    grad_pre = grad_pre_of(cot, slope_ref, wtt_ref)
    late_ref[:, :SLICE] = grad_pre.astype(F32).T.astype(BF16).reshape(FRAMES, SLICE, CELLS)
    late_ref[:, SLICE:] = cot[0].astype(F32).T.astype(BF16).reshape(FRAMES, SLICE, CELLS)
    cot_ref[...] = cot[0]
    pre_ref[...] = grad_pre


def spread_kernel(cot_ref, pre_ref, wst_ref, gin_ref):
    gin_ref[...] = spread_of(cot_ref[...], pre_ref[...], wst_ref)


def small(kernel, outs, args, specs, flops, read):
    return pl.pallas_call(
        kernel,
        out_shape=tuple(jax.ShapeDtypeStruct(o, BF16) for o in outs),
        in_specs=specs,
        out_specs=(VMEM,) * len(outs),
        compiler_params=pltpu.CompilerParams(vmem_limit_bytes=16 << 20),
        cost_estimate=pl.CostEstimate(flops=flops, bytes_accessed=read, transcendentals=0),
    )(*args)


def pack_kernel(*refs):
    pieces, out, sems = refs[:8], refs[8], refs[9]
    copies = [pltpu.make_async_copy(pieces[k], out.at[k], sems.at[k]) for k in range(8)]
    for c in copies:
        c.start()
    for c in copies:
        c.wait()


def pack(pieces):
    return pl.pallas_call(
        pack_kernel,
        name="pack",
        out_shape=jax.ShapeDtypeStruct((8,) + pieces[0].shape, BF16),
        in_specs=[ANY] * 8,
        out_specs=ANY,
        scratch_shapes=[pltpu.SemaphoreType.DMA((8,))],
        compiler_params=pltpu.CompilerParams(vmem_limit_bytes=4 << 20),
        cost_estimate=pl.CostEstimate(flops=0, bytes_accessed=4000000, transcendentals=0),
    )(*pieces)


def weights_kernel(late_ref, *refs):
    ring = refs[:8]
    swapped = refs[8]
    outs = refs[9:13]
    x, act, left, result, sems = refs[13:]
    seq, d = lax.axis_index("seq"), lax.axis_index("dp")
    z, core = seq // 2, seq % 2
    half = FRAMES // 2
    copies = []
    for k in range(half):
        chip = lax.rem(z + k, half)
        for which, source in ((core, ring[k]), (1 - core, swapped.at[k])):
            t = pl.multiple_of((2 * chip + which) * CELLS, CELLS)
            for part, target in ((0, x), (1, act)):
                n = len(copies)
                c = pltpu.make_async_copy(source.at[part], target.at[:, pl.ds(t, CELLS)], sems.at[n])
                c.start()
                copies.append(c)
    g = late_ref[:, :SLICE].astype(F32).reshape(FRAMES * SLICE, CELLS)
    lane = lax.broadcasted_iota(jnp.int32, g.shape, 1)
    row, col = lane // COLS, lane % COLS
    for r in range(3):
        for q in range(3):
            dr, dc = r - 1, q - 1
            v = g if dr == 0 and dc == 0 else pltpu.roll(g, (dr * COLS + dc) % CELLS, 1)
            keep = None
            for at, step, size in ((row, dr, ROWS), (col, dc, COLS)):
                if step:
                    good = (at != 0) if step > 0 else (at != size - 1)
                    keep = good if keep is None else keep & good
            if keep is not None:
                v = jnp.where(keep, v, 0.0)
            v = v.astype(BF16).reshape(FRAMES, SLICE, CELLS)
            base = (3 * r + q) * SLICE
            for f in range(FRAMES):
                left[base : base + SLICE, f * CELLS : (f + 1) * CELLS] = v[f]
    for k in range(3):
        base = (9 + k) * SLICE
        for f in range(FRAMES):
            if f + k < FRAMES:
                v = late_ref[f + k, SLICE:]
            else:
                v = jnp.zeros((SLICE, CELLS), BF16)
            left[base : base + SLICE, f * CELLS : (f + 1) * CELLS] = v
    for c in copies:
        c.wait()
    spatial = nt(x[...], left[: 9 * SLICE])
    temporal = nt(act[...], left[9 * SLICE :])
    result[:, :, :, : 9 * SLICE] = spatial.reshape(FRAMES, CLIPS, SUB, 9 * SLICE)
    result[:, :, :, 9 * SLICE :] = temporal.reshape(FRAMES, CLIPS, SUB, 3 * SLICE)
    for k in range(CLIPS):
        outs[k][...] = result[:, lax.rem(d + k, CLIPS)].astype(BF16)


def weights(late, ring, swapped):
    return pl.pallas_call(
        weights_kernel,
        name="weight_grads",
        out_shape=(jax.ShapeDtypeStruct((FRAMES, SUB, WIDE), BF16),) * CLIPS,
        in_specs=[VMEM] + [ANY] * 9,
        out_specs=(VMEM,) * CLIPS,
        scratch_shapes=[
            pltpu.VMEM((CH, FRAMES * CELLS), BF16),
            pltpu.VMEM((CH, FRAMES * CELLS), BF16),
            pltpu.VMEM((WIDE, FRAMES * CELLS), BF16),
            pltpu.VMEM((FRAMES, CLIPS, SUB, WIDE), F32),
            pltpu.SemaphoreType.DMA((4 * FRAMES // 2,)),
        ],
        compiler_params=pltpu.CompilerParams(vmem_limit_bytes=24 << 20),
        cost_estimate=pl.CostEstimate(flops=1610000000, bytes_accessed=5000000, transcendentals=0),
    )(late, *ring, swapped)


def assemble_kernel(*refs):
    parts, (spatial_ref, temporal_ref) = refs[:CLIPS], refs[CLIPS:]
    d = lax.axis_index("dp")
    for k in range(CLIPS):
        source = lax.rem(d + CLIPS - k, CLIPS)
        rows = pl.ds(pl.multiple_of(source * SUB, SUB), SUB)
        part = parts[k][...].astype(F32)
        for tap in range(TAPS):
            line = jnp.concatenate(
                [part[s, :, tap * SLICE : (tap + 1) * SLICE] for s in range(FRAMES)], axis=-1
            )
            if tap < 9:
                spatial_ref[tap, rows, :] = line
            else:
                temporal_ref[tap - 9, rows, :] = line


def assemble(parts):
    return pl.pallas_call(
        assemble_kernel,
        name="assemble",
        out_shape=(
            jax.ShapeDtypeStruct((9, SLICE, CH), F32),
            jax.ShapeDtypeStruct((3, SLICE, CH), F32),
        ),
        in_specs=[VMEM] * CLIPS,
        out_specs=(VMEM, VMEM),
        compiler_params=pltpu.CompilerParams(vmem_limit_bytes=24 << 20),
        cost_estimate=pl.CostEstimate(flops=1000000, bytes_accessed=1200000, transcendentals=0),
    )(*parts)


def send(value, axes, sizes, step):
    n, m = sizes
    pairs = [
        (a * m + b, (a + step[0]) % n * m + (b + step[1]) % m) for a in range(n) for b in range(m)
    ]
    return lax.ppermute(value, axes, pairs)


def around(value, axis, size, step):
    return lax.ppermute(value, axis, [(i, (i + step) % size) for i in range(size)])


def local(sizes, *args):
    return backward(sizes, *args)


def backward(sizes, section_inputs, w_spatial, w_temporal, grad_output, frame_start, frame_count):
    axes = ("pipe", "seq")
    steps = sizes[0]
    x = section_inputs.reshape(CELLS, CH)
    ws, wt = w_spatial[0], w_temporal[0]
    cot = grad_output.reshape(CELLS, CH)
    ahead2 = send(cot, axes, sizes, (0, -2))
    ahead1 = send(cot, axes, sizes, (0, -1))
    mine, slope, wtt, wst = forward(x, wt, ws)
    head = [frame_start, frame_count, cot, ahead1, ahead2]
    head_specs = [SMEM, SMEM] + [VMEM] * 3
    ring = {0: mine}
    half = FRAMES // 2

    def grow(k):
        ring[-k] = around(ring[1 - k], "seq", FRAMES, 2)
        if k < half // 2:
            ring[k] = around(ring[k - 1], "seq", FRAMES, -2)

    grow(1)
    got = []
    for step in range(steps - 1):
        (grad_in,) = small(
            functools.partial(section_kernel, len(got)),
            [(CELLS, CH)],
            head + got + [slope, wtt, wst],
            head_specs + [VMEM] * (len(got) + 3),
            805000000,
            7000000,
        )
        got = [send(grad_in, axes, sizes, (-1, -k)) for k in (2, 1, 0)][::-1]
        grow(step + 2)
    late, cot0, grad_pre = small(
        functools.partial(emit_kernel, len(got)),
        [(FRAMES, 2 * SLICE, CELLS), (CELLS, CH), (CELLS, CH)],
        head + got + [slope, wtt],
        head_specs + [VMEM] * (len(got) + 2),
        200000000,
        2000000,
    )
    gathered = lax.all_to_all(late, "seq", 0, 0, tiled=True)
    pieces = [ring[k if k < half // 2 else k - half] for k in range(half)]
    packed = pack(pieces)
    swapped = lax.ppermute(packed, "seq", [(i, i ^ 1) for i in range(FRAMES)])
    (grad_in,) = small(
        spread_kernel, [(CELLS, CH)], [cot0, grad_pre, wst], [VMEM] * 3, 604000000, 5000000
    )
    partial = weights(gathered, pieces, swapped)
    shares = [partial[0]] + [around(partial[k], "dp", CLIPS, k) for k in (1, 2, 3)]
    share = sum(s.astype(F32) for s in shares).astype(BF16)
    share = lax.all_to_all(share, "seq", 0, 0, tiled=True)
    parts = [share] + [around(share, "dp", CLIPS, k) for k in (1, 2, 3)]
    spatial, temporal = assemble(parts)
    return grad_in.reshape(section_inputs.shape), spatial[None], temporal[None]


def solution(mesh):
    sizes = (mesh.shape["pipe"], mesh.shape["seq"])
    placed = (
        P("pipe", "dp", "seq", None, None, None),
        P("pipe", None, None, None),
        P("pipe", None, None, None),
        P("dp", "seq", None, None, None),
        P("dp"),
        P("dp"),
    )
    return jax.shard_map(
        functools.partial(local, sizes),
        mesh=mesh,
        in_specs=placed,
        out_specs=(
            P("pipe", "dp", "seq", None, None, None),
            P("pipe", None, "seq", None),
            P("pipe", None, "seq", None),
        ),
        check_vma=False,
    )
```

```python
import functools

import jax
import jax.numpy as jnp
from jax import lax
from jax.experimental import pallas as pl
from jax.experimental.pallas import tpu as pltpu
from jax.sharding import PartitionSpec as P


F32 = jnp.float32
BF16 = jnp.bfloat16
ANY = pl.BlockSpec(memory_space=pl.ANY)
SMEM = pl.BlockSpec(memory_space=pltpu.SMEM)
VMEM = pl.BlockSpec(memory_space=pltpu.VMEM)
HBM = pl.BlockSpec(memory_space=pltpu.HBM)

ROWS, COLS, CH = 16, 8, 512
CELLS = ROWS * COLS
FRAMES = 16
CLIPS = 4
SLICE = CH // FRAMES
TAPS = 12
WIDE = TAPS * SLICE
SUB = SLICE // CLIPS


def nn(a, b):
    return lax.dot_general(a, b, (((1,), (0,)), ((), ())), preferred_element_type=F32)


def nt(a, b):
    return lax.dot_general(a, b, (((1,), (1,)), ((), ())), preferred_element_type=F32)


def column_shifts(v):
    col = lax.broadcasted_iota(jnp.int32, v.shape, 0) % COLS
    before = jnp.where(col == 0, 0.0, pltpu.roll(v, 1, 0))
    after = jnp.where(col == COLS - 1, 0.0, pltpu.roll(v, CELLS - 1, 0))
    return {0: v, -1: before, 1: after}


def row_shift(v, step):
    zero = jnp.zeros((COLS, v.shape[1]), v.dtype)
    if step == 0:
        return v
    if step < 0:
        return jnp.concatenate([zero, v[:-COLS]], axis=0)
    return jnp.concatenate([v[COLS:], zero], axis=0)


def forward_kernel(
    x_hbm, wt_hbm, ws_hbm, mine_ref, slope_ref, wtt_ref, wst_ref, x_ref, wt, ws, sems
):
    fetch = pltpu.make_async_copy(x_hbm, x_ref, sems.at[TAPS])
    fetch.start()
    copies = [pltpu.make_async_copy(ws_hbm.at[k], ws.at[k], sems.at[k]) for k in range(9)]
    copies += [pltpu.make_async_copy(wt_hbm.at[k], wt.at[k], sems.at[9 + k]) for k in range(3)]
    for c in copies:
        c.start()
    fetch.wait()
    x = x_ref[...].astype(F32)
    cols = column_shifts(x)
    mine_ref[0] = x.T.astype(BF16)
    pre = None
    for r in range(3):
        for q in range(3):
            k = 3 * r + q
            lhs = row_shift(cols[q - 1], r - 1).astype(BF16)
            copies[k].wait()
            term = nn(lhs, ws[k])
            pre = term if pre is None else pre + term
            wst_ref[k] = ws[k].T
    s = jax.nn.sigmoid(pre)
    slope_ref[...] = s * (1.0 + pre * (1.0 - s))
    mine_ref[1] = (pre * s).astype(BF16).astype(F32).T.astype(BF16)
    for k in range(3):
        copies[9 + k].wait()
        wtt_ref[k] = wt[k].T


def forward(x, wt, ws):
    return pl.pallas_call(
        forward_kernel,
        name="block_forward",
        out_shape=(
            jax.ShapeDtypeStruct((2, CH, CELLS), BF16),
            jax.ShapeDtypeStruct((CELLS, CH), F32),
            jax.ShapeDtypeStruct((3, CH, CH), BF16),
            jax.ShapeDtypeStruct((9, CH, CH), BF16),
        ),
        in_specs=[HBM] * 3,
        out_specs=(VMEM,) * 4,
        scratch_shapes=[
            pltpu.VMEM((CELLS, CH), BF16),
            pltpu.VMEM((3, CH, CH), BF16),
            pltpu.VMEM((9, CH, CH), BF16),
            pltpu.SemaphoreType.DMA((TAPS + 1,)),
        ],
        compiler_params=pltpu.CompilerParams(vmem_limit_bytes=24 << 20),
        cost_estimate=pl.CostEstimate(flops=1208000000, bytes_accessed=13000000, transcendentals=65536),
    )(*(pltpu.with_memory_space_constraint(v, pltpu.HBM) for v in (x, wt, ws)))


def cotangents(count, refs):
    start_ref, count_ref = refs[0], refs[1]
    own = refs[2:5]
    got = refs[5 : 5 + count]
    seq = lax.axis_index("seq")
    last = lax.axis_index("pipe") == lax.axis_size("pipe") - 1
    out = []
    for k in range(3):
        t = seq + k
        counted = (t >= start_ref[0]) & (t < count_ref[0])
        if count:
            value = jnp.where(last, own[k][...], got[k][...])
            keep = jnp.where(last, counted, t < FRAMES)
        else:
            value, keep = own[k][...], counted
        out.append(jnp.where(keep, value, jnp.zeros((CELLS, CH), BF16)))
    return out, refs[5 + count :]


def grad_pre_of(cot, slope_ref, wtt_ref):
    grad_act = nn(cot[0], wtt_ref[0]) + nn(cot[1], wtt_ref[1]) + nn(cot[2], wtt_ref[2])
    return (grad_act.astype(BF16).astype(F32) * slope_ref[...]).astype(BF16)


def spread_of(cot, grad_pre, wst_ref):
    cols = column_shifts(grad_pre.astype(F32))
    total = cot.astype(F32)
    for r in range(3):
        for q in range(3):
            lhs = row_shift(cols[1 - q], 1 - r).astype(BF16)
            total = total + nn(lhs, wst_ref[3 * r + q])
    return total.astype(BF16)


def section_kernel(count, *refs):
    cot, (slope_ref, wtt_ref, wst_ref, gin_ref) = cotangents(count, refs)
    grad_pre = grad_pre_of(cot, slope_ref, wtt_ref)
    gin_ref[...] = spread_of(cot[0], grad_pre, wst_ref)


def emit_kernel(count, *refs):
    cot, (slope_ref, wtt_ref, late_ref, cot_ref, pre_ref) = cotangents(count, refs)
    grad_pre = grad_pre_of(cot, slope_ref, wtt_ref)
    late_ref[:, :SLICE] = grad_pre.astype(F32).T.astype(BF16).reshape(FRAMES, SLICE, CELLS)
    late_ref[:, SLICE:] = cot[0].astype(F32).T.astype(BF16).reshape(FRAMES, SLICE, CELLS)
    cot_ref[...] = cot[0]
    pre_ref[...] = grad_pre


def spread_kernel(cot_ref, pre_ref, wst_ref, gin_ref):
    gin_ref[...] = spread_of(cot_ref[...], pre_ref[...], wst_ref)


def small(kernel, outs, args, specs, flops, read):
    return pl.pallas_call(
        kernel,
        out_shape=tuple(jax.ShapeDtypeStruct(o, BF16) for o in outs),
        in_specs=specs,
        out_specs=(VMEM,) * len(outs),
        compiler_params=pltpu.CompilerParams(vmem_limit_bytes=16 << 20),
        cost_estimate=pl.CostEstimate(flops=flops, bytes_accessed=read, transcendentals=0),
    )(*args)


def pack_kernel(*refs):
    pieces, out, sems = refs[:8], refs[8], refs[9]
    copies = [pltpu.make_async_copy(pieces[k], out.at[k], sems.at[k]) for k in range(8)]
    for c in copies:
        c.start()
    for c in copies:
        c.wait()


def pack(pieces):
    return pl.pallas_call(
        pack_kernel,
        name="pack",
        out_shape=jax.ShapeDtypeStruct((8,) + pieces[0].shape, BF16),
        in_specs=[ANY] * 8,
        out_specs=ANY,
        scratch_shapes=[pltpu.SemaphoreType.DMA((8,))],
        compiler_params=pltpu.CompilerParams(vmem_limit_bytes=4 << 20),
        cost_estimate=pl.CostEstimate(flops=0, bytes_accessed=4000000, transcendentals=0),
    )(*pieces)


def weights_kernel(late_ref, *refs):
    ring = refs[:8]
    swapped = refs[8]
    outs = refs[9:13]
    left, result = refs[13:]
    seq, d = lax.axis_index("seq"), lax.axis_index("dp")
    z, core = seq // 2, seq % 2
    half = FRAMES // 2
    frame = []
    for k in range(half):
        chip = lax.rem(z + k, half)
        frame += [2 * chip + core, 2 * chip + 1 - core]
    g = jnp.stack([late_ref[t, :SLICE] for t in frame]).astype(F32).reshape(FRAMES * SLICE, CELLS)
    lane = lax.broadcasted_iota(jnp.int32, g.shape, 1)
    row, col = lane // COLS, lane % COLS
    for r in range(3):
        for q in range(3):
            dr, dc = r - 1, q - 1
            v = g if dr == 0 and dc == 0 else pltpu.roll(g, (dr * COLS + dc) % CELLS, 1)
            keep = None
            for at, step, size in ((row, dr, ROWS), (col, dc, COLS)):
                if step:
                    good = (at != 0) if step > 0 else (at != size - 1)
                    keep = good if keep is None else keep & good
            if keep is not None:
                v = jnp.where(keep, v, 0.0)
            v = v.astype(BF16).reshape(FRAMES, SLICE, CELLS)
            base = (3 * r + q) * SLICE
            for f in range(FRAMES):
                left[base : base + SLICE, f * CELLS : (f + 1) * CELLS] = v[f]
    for k in range(3):
        base = (9 + k) * SLICE
        for f in range(FRAMES):
            t = frame[f] + k
            v = late_ref[jnp.minimum(t, FRAMES - 1), SLICE:]
            if k:
                v = jnp.where(t < FRAMES, v, jnp.zeros((SLICE, CELLS), BF16))
            left[base : base + SLICE, f * CELLS : (f + 1) * CELLS] = v
    spatial = temporal = None
    for k in range(half):
        here = slice(2 * k * CELLS, 2 * (k + 1) * CELLS)
        x = jnp.concatenate([ring[k][0], swapped[k, 0]], axis=1)
        act = jnp.concatenate([ring[k][1], swapped[k, 1]], axis=1)
        more = nt(x, left[: 9 * SLICE, here])
        spatial = more if spatial is None else spatial + more
        more = nt(act, left[9 * SLICE :, here])
        temporal = more if temporal is None else temporal + more
    result[:, :, :, : 9 * SLICE] = spatial.reshape(FRAMES, CLIPS, SUB, 9 * SLICE)
    result[:, :, :, 9 * SLICE :] = temporal.reshape(FRAMES, CLIPS, SUB, 3 * SLICE)
    for k in range(CLIPS):
        outs[k][...] = result[:, lax.rem(d + k, CLIPS)].astype(BF16)


def weights(late, ring, swapped):
    return pl.pallas_call(
        weights_kernel,
        name="weight_grads",
        out_shape=(jax.ShapeDtypeStruct((FRAMES, SUB, WIDE), BF16),) * CLIPS,
        in_specs=[VMEM] * 10,
        out_specs=(VMEM,) * CLIPS,
        scratch_shapes=[
            pltpu.VMEM((WIDE, FRAMES * CELLS), BF16),
            pltpu.VMEM((FRAMES, CLIPS, SUB, WIDE), F32),
        ],
        compiler_params=pltpu.CompilerParams(vmem_limit_bytes=24 << 20),
        cost_estimate=pl.CostEstimate(flops=1610000000, bytes_accessed=5000000, transcendentals=0),
    )(late, *ring, swapped)


def assemble_kernel(*refs):
    parts, (spatial_ref, temporal_ref) = refs[:CLIPS], refs[CLIPS:]
    d = lax.axis_index("dp")
    for k in range(CLIPS):
        source = lax.rem(d + CLIPS - k, CLIPS)
        rows = pl.ds(pl.multiple_of(source * SUB, SUB), SUB)
        part = parts[k][...].astype(F32)
        for tap in range(TAPS):
            line = jnp.concatenate(
                [part[s, :, tap * SLICE : (tap + 1) * SLICE] for s in range(FRAMES)], axis=-1
            )
            if tap < 9:
                spatial_ref[tap, rows, :] = line
            else:
                temporal_ref[tap - 9, rows, :] = line


def assemble(parts):
    return pl.pallas_call(
        assemble_kernel,
        name="assemble",
        out_shape=(
            jax.ShapeDtypeStruct((9, SLICE, CH), F32),
            jax.ShapeDtypeStruct((3, SLICE, CH), F32),
        ),
        in_specs=[VMEM] * CLIPS,
        out_specs=(VMEM, VMEM),
        compiler_params=pltpu.CompilerParams(vmem_limit_bytes=24 << 20),
        cost_estimate=pl.CostEstimate(flops=1000000, bytes_accessed=1200000, transcendentals=0),
    )(*parts)


def send(value, axes, sizes, step):
    n, m = sizes
    pairs = [
        (a * m + b, (a + step[0]) % n * m + (b + step[1]) % m) for a in range(n) for b in range(m)
    ]
    return lax.ppermute(value, axes, pairs)


def around(value, axis, size, step):
    return lax.ppermute(value, axis, [(i, (i + step) % size) for i in range(size)])


def local(sizes, *args):
    return backward(sizes, *args)


def backward(sizes, section_inputs, w_spatial, w_temporal, grad_output, frame_start, frame_count):
    axes = ("pipe", "seq")
    steps = sizes[0]
    x = section_inputs.reshape(CELLS, CH)
    ws, wt = w_spatial[0], w_temporal[0]
    cot = grad_output.reshape(CELLS, CH)
    ahead2 = send(cot, axes, sizes, (0, -2))
    ahead1 = send(cot, axes, sizes, (0, -1))
    mine, slope, wtt, wst = forward(x, wt, ws)
    frame_start, frame_count, slope = lax.optimization_barrier((frame_start, frame_count, slope))
    head = [frame_start, frame_count, cot, ahead1, ahead2]
    head_specs = [SMEM, SMEM] + [VMEM] * 3
    ring = {0: mine}
    half = FRAMES // 2

    def grow(k):
        ring[-k] = around(ring[1 - k], "seq", FRAMES, 2)
        if k < half // 2:
            ring[k] = around(ring[k - 1], "seq", FRAMES, -2)

    grow(1)
    got = []
    for step in range(steps - 1):
        (grad_in,) = small(
            functools.partial(section_kernel, len(got)),
            [(CELLS, CH)],
            head + got + [slope, wtt, wst],
            head_specs + [VMEM] * (len(got) + 3),
            805000000,
            7000000,
        )
        got = [send(grad_in, axes, sizes, (-1, -k)) for k in (2, 1, 0)][::-1]
        grow(step + 2)
    late, cot0, grad_pre = small(
        functools.partial(emit_kernel, len(got)),
        [(FRAMES, 2 * SLICE, CELLS), (CELLS, CH), (CELLS, CH)],
        head + got + [slope, wtt],
        head_specs + [VMEM] * (len(got) + 2),
        200000000,
        2000000,
    )
    gathered = lax.all_to_all(late, "seq", 0, 0, tiled=True)
    pieces = [ring[k if k < half // 2 else k - half] for k in range(half)]
    packed = pack(pieces)
    swapped = lax.ppermute(packed, "seq", [(i, i ^ 1) for i in range(FRAMES)])
    (grad_in,) = small(
        spread_kernel, [(CELLS, CH)], [cot0, grad_pre, wst], [VMEM] * 3, 604000000, 5000000
    )
    partial = weights(gathered, pieces, swapped)
    shares = [partial[0]] + [around(partial[k], "dp", CLIPS, k) for k in (1, 2, 3)]
    share = sum(s.astype(F32) for s in shares).astype(BF16)
    share = lax.all_to_all(share, "seq", 0, 0, tiled=True)
    parts = [share] + [around(share, "dp", CLIPS, k) for k in (1, 2, 3)]
    spatial, temporal = assemble(parts)
    return grad_in.reshape(section_inputs.shape), spatial[None], temporal[None]


def solution(mesh):
    sizes = (mesh.shape["pipe"], mesh.shape["seq"])
    placed = (
        P("pipe", "dp", "seq", None, None, None),
        P("pipe", None, None, None),
        P("pipe", None, None, None),
        P("dp", "seq", None, None, None),
        P("dp"),
        P("dp"),
    )
    return jax.shard_map(
        functools.partial(local, sizes),
        mesh=mesh,
        in_specs=placed,
        out_specs=(
            P("pipe", "dp", "seq", None, None, None),
            P("pipe", None, "seq", None),
            P("pipe", None, "seq", None),
        ),
        check_vma=False,
    )
```

```python
import functools

import jax
import jax.numpy as jnp
from jax import lax
from jax.experimental import pallas as pl
from jax.experimental.pallas import tpu as pltpu
from jax.sharding import PartitionSpec as P


F32 = jnp.float32
BF16 = jnp.bfloat16
ANY = pl.BlockSpec(memory_space=pl.ANY)
SMEM = pl.BlockSpec(memory_space=pltpu.SMEM)
VMEM = pl.BlockSpec(memory_space=pltpu.VMEM)
HBM = pl.BlockSpec(memory_space=pltpu.HBM)

ROWS, COLS, CH = 16, 8, 512
CELLS = ROWS * COLS
FRAMES = 16
CLIPS = 4
SLICE = CH // FRAMES
TAPS = 12
WIDE = TAPS * SLICE
SUB = SLICE // CLIPS


def nn(a, b):
    return lax.dot_general(a, b, (((1,), (0,)), ((), ())), preferred_element_type=F32)


def nt(a, b):
    return lax.dot_general(a, b, (((1,), (1,)), ((), ())), preferred_element_type=F32)


def column_shifts(v):
    col = lax.broadcasted_iota(jnp.int32, v.shape, 0) % COLS
    before = jnp.where(col == 0, 0.0, pltpu.roll(v, 1, 0))
    after = jnp.where(col == COLS - 1, 0.0, pltpu.roll(v, CELLS - 1, 0))
    return {0: v, -1: before, 1: after}


def row_shift(v, step):
    zero = jnp.zeros((COLS, v.shape[1]), v.dtype)
    if step == 0:
        return v
    if step < 0:
        return jnp.concatenate([zero, v[:-COLS]], axis=0)
    return jnp.concatenate([v[COLS:], zero], axis=0)


def forward_kernel(
    x_hbm, wt_hbm, ws_hbm, start_ref, count_ref, mine_ref, slope_ref, wtt_ref, wst_ref, keep_ref,
    x_ref, wt, ws, sems
):
    fetch = pltpu.make_async_copy(x_hbm, x_ref, sems.at[TAPS])
    fetch.start()
    copies = [pltpu.make_async_copy(ws_hbm.at[k], ws.at[k], sems.at[k]) for k in range(9)]
    copies += [pltpu.make_async_copy(wt_hbm.at[k], wt.at[k], sems.at[9 + k]) for k in range(3)]
    for c in copies:
        c.start()
    fetch.wait()
    x = x_ref[...].astype(F32)
    cols = column_shifts(x)
    mine_ref[0] = x.T.astype(BF16)
    pre = None
    for r in range(3):
        for q in range(3):
            k = 3 * r + q
            lhs = row_shift(cols[q - 1], r - 1).astype(BF16)
            copies[k].wait()
            term = nn(lhs, ws[k])
            pre = term if pre is None else pre + term
            wst_ref[k] = ws[k].T
    s = jax.nn.sigmoid(pre)
    slope_ref[...] = s * (1.0 + pre * (1.0 - s))
    mine_ref[1] = (pre * s).astype(BF16).astype(F32).T.astype(BF16)
    for k in range(3):
        copies[9 + k].wait()
        wtt_ref[k] = wt[k].T
    seq = lax.axis_index("seq")
    last = lax.axis_index("pipe") == lax.axis_size("pipe") - 1
    t = seq + lax.broadcasted_iota(jnp.int32, (8, CH), 0)
    low = jnp.where(last, start_ref[0], 0)
    high = jnp.where(last, count_ref[0], FRAMES)
    keep_ref[...] = ((t >= low) & (t < high)).astype(F32)


def forward(x, wt, ws, start, count):
    return pl.pallas_call(
        forward_kernel,
        name="block_forward",
        out_shape=(
            jax.ShapeDtypeStruct((2, CH, CELLS), BF16),
            jax.ShapeDtypeStruct((CELLS, CH), F32),
            jax.ShapeDtypeStruct((3, CH, CH), BF16),
            jax.ShapeDtypeStruct((9, CH, CH), BF16),
            jax.ShapeDtypeStruct((8, CH), F32),
        ),
        in_specs=[HBM] * 3 + [SMEM] * 2,
        out_specs=(VMEM,) * 5,
        scratch_shapes=[
            pltpu.VMEM((CELLS, CH), BF16),
            pltpu.VMEM((3, CH, CH), BF16),
            pltpu.VMEM((9, CH, CH), BF16),
            pltpu.SemaphoreType.DMA((TAPS + 1,)),
        ],
        compiler_params=pltpu.CompilerParams(vmem_limit_bytes=24 << 20),
        cost_estimate=pl.CostEstimate(flops=1208000000, bytes_accessed=13000000, transcendentals=65536),
    )(*(pltpu.with_memory_space_constraint(v, pltpu.HBM) for v in (x, wt, ws)), start, count)


def cotangents(count, refs):
    keep_ref = refs[0]
    own = refs[1:4]
    got = refs[4 : 4 + count]
    last = lax.axis_index("pipe") == lax.axis_size("pipe") - 1
    out = []
    for k in range(3):
        value = own[k][...]
        if count:
            value = jnp.where(last, value, got[k][...])
        keep = keep_ref[k : k + 1, :] != 0.0
        out.append(jnp.where(keep, value.astype(F32), 0.0).astype(BF16))
    return out, refs[4 + count :]


def grad_pre_of(cot, slope_ref, wtt_ref):
    grad_act = nn(cot[0], wtt_ref[0]) + nn(cot[1], wtt_ref[1]) + nn(cot[2], wtt_ref[2])
    return (grad_act.astype(BF16).astype(F32) * slope_ref[...]).astype(BF16)


def spread_of(cot, grad_pre, wst_ref):
    cols = column_shifts(grad_pre.astype(F32))
    total = cot.astype(F32)
    for r in range(3):
        for q in range(3):
            lhs = row_shift(cols[1 - q], 1 - r).astype(BF16)
            total = total + nn(lhs, wst_ref[3 * r + q])
    return total.astype(BF16)


def section_kernel(count, *refs):
    cot, (slope_ref, wtt_ref, wst_ref, gin_ref) = cotangents(count, refs)
    grad_pre = grad_pre_of(cot, slope_ref, wtt_ref)
    gin_ref[...] = spread_of(cot[0], grad_pre, wst_ref)


def emit_kernel(count, *refs):
    cot, (slope_ref, wtt_ref, late_ref, cot_ref, pre_ref) = cotangents(count, refs)
    grad_pre = grad_pre_of(cot, slope_ref, wtt_ref)
    late_ref[:, :SLICE] = grad_pre.astype(F32).T.astype(BF16).reshape(FRAMES, SLICE, CELLS)
    late_ref[:, SLICE:] = cot[0].astype(F32).T.astype(BF16).reshape(FRAMES, SLICE, CELLS)
    cot_ref[...] = cot[0]
    pre_ref[...] = grad_pre


def spread_kernel(cot_ref, pre_ref, wst_ref, gin_ref):
    gin_ref[...] = spread_of(cot_ref[...], pre_ref[...], wst_ref)


def pick_kernel(two_ref, none_ref, out_ref):
    first = lax.axis_index("seq") % 2 == 0
    out_ref[...] = jnp.where(first, two_ref[...], none_ref[...])


def small(kernel, outs, args, specs, flops, read):
    return pl.pallas_call(
        kernel,
        out_shape=tuple(jax.ShapeDtypeStruct(o, BF16) for o in outs),
        in_specs=specs,
        out_specs=(VMEM,) * len(outs),
        compiler_params=pltpu.CompilerParams(vmem_limit_bytes=16 << 20),
        cost_estimate=pl.CostEstimate(flops=flops, bytes_accessed=read, transcendentals=0),
    )(*args)


def pack_kernel(*refs):
    pieces, out, sems = refs[:8], refs[8], refs[9]
    copies = [pltpu.make_async_copy(pieces[k], out.at[k], sems.at[k]) for k in range(8)]
    for c in copies:
        c.start()
    for c in copies:
        c.wait()


def pack(pieces):
    return pl.pallas_call(
        pack_kernel,
        name="pack",
        out_shape=jax.ShapeDtypeStruct((8,) + pieces[0].shape, BF16),
        in_specs=[ANY] * 8,
        out_specs=ANY,
        scratch_shapes=[pltpu.SemaphoreType.DMA((8,))],
        compiler_params=pltpu.CompilerParams(vmem_limit_bytes=4 << 20),
        cost_estimate=pl.CostEstimate(flops=0, bytes_accessed=4000000, transcendentals=0),
    )(*pieces)


def tick_kernel(keep_ref, out_ref):
    out_ref[...] = keep_ref[...]


def tick(keep):
    return pl.pallas_call(
        tick_kernel,
        out_shape=jax.ShapeDtypeStruct(keep.shape, keep.dtype),
        in_specs=[VMEM],
        out_specs=VMEM,
        compiler_params=pltpu.CompilerParams(vmem_limit_bytes=1 << 20),
        cost_estimate=pl.CostEstimate(flops=0, bytes_accessed=32768, transcendentals=0),
    )(keep)


def weights_kernel(late_ref, *refs):
    ring = refs[:8]
    swapped = refs[8]
    outs = refs[9:13]
    left, result = refs[13:]
    seq, d = lax.axis_index("seq"), lax.axis_index("dp")
    z, core = seq // 2, seq % 2
    half = FRAMES // 2
    frame = []
    for k in range(half):
        chip = lax.rem(z + k, half)
        frame += [2 * chip + core, 2 * chip + 1 - core]
    g = jnp.stack([late_ref[t, :SLICE] for t in frame]).astype(F32).reshape(FRAMES * SLICE, CELLS)
    lane = lax.broadcasted_iota(jnp.int32, g.shape, 1)
    row, col = lane // COLS, lane % COLS
    for r in range(3):
        for q in range(3):
            dr, dc = r - 1, q - 1
            v = g if dr == 0 and dc == 0 else pltpu.roll(g, (dr * COLS + dc) % CELLS, 1)
            keep = None
            for at, step, size in ((row, dr, ROWS), (col, dc, COLS)):
                if step:
                    good = (at != 0) if step > 0 else (at != size - 1)
                    keep = good if keep is None else keep & good
            if keep is not None:
                v = jnp.where(keep, v, 0.0)
            v = v.astype(BF16).reshape(FRAMES, SLICE, CELLS)
            base = (3 * r + q) * SLICE
            for f in range(FRAMES):
                left[base : base + SLICE, f * CELLS : (f + 1) * CELLS] = v[f]
    for k in range(3):
        base = (9 + k) * SLICE
        for f in range(FRAMES):
            t = frame[f] + k
            v = late_ref[jnp.minimum(t, FRAMES - 1), SLICE:]
            if k:
                v = jnp.where(t < FRAMES, v, jnp.zeros((SLICE, CELLS), BF16))
            left[base : base + SLICE, f * CELLS : (f + 1) * CELLS] = v
    spatial = temporal = None
    for k in range(half):
        here = slice(2 * k * CELLS, 2 * (k + 1) * CELLS)
        x = jnp.concatenate([ring[k][0], swapped[k, 0]], axis=1)
        act = jnp.concatenate([ring[k][1], swapped[k, 1]], axis=1)
        more = nt(x, left[: 9 * SLICE, here])
        spatial = more if spatial is None else spatial + more
        more = nt(act, left[9 * SLICE :, here])
        temporal = more if temporal is None else temporal + more
    result[:, :, :, : 9 * SLICE] = spatial.reshape(FRAMES, CLIPS, SUB, 9 * SLICE)
    result[:, :, :, 9 * SLICE :] = temporal.reshape(FRAMES, CLIPS, SUB, 3 * SLICE)
    for k in range(CLIPS):
        outs[k][...] = result[:, lax.rem(d + k, CLIPS)].astype(BF16)


def weights(late, ring, swapped):
    return pl.pallas_call(
        weights_kernel,
        name="weight_grads",
        out_shape=(jax.ShapeDtypeStruct((FRAMES, SUB, WIDE), BF16),) * CLIPS,
        in_specs=[VMEM] * 10,
        out_specs=(VMEM,) * CLIPS,
        scratch_shapes=[
            pltpu.VMEM((WIDE, FRAMES * CELLS), BF16),
            pltpu.VMEM((FRAMES, CLIPS, SUB, WIDE), F32),
        ],
        compiler_params=pltpu.CompilerParams(vmem_limit_bytes=24 << 20),
        cost_estimate=pl.CostEstimate(flops=1610000000, bytes_accessed=5000000, transcendentals=0),
    )(late, *ring, swapped)


def assemble_kernel(*refs):
    parts, (spatial_ref, temporal_ref) = refs[:CLIPS], refs[CLIPS:]
    d = lax.axis_index("dp")
    for k in range(CLIPS):
        source = lax.rem(d + CLIPS - k, CLIPS)
        rows = pl.ds(pl.multiple_of(source * SUB, SUB), SUB)
        part = parts[k][...].astype(F32)
        for tap in range(TAPS):
            line = jnp.concatenate(
                [part[s, :, tap * SLICE : (tap + 1) * SLICE] for s in range(FRAMES)], axis=-1
            )
            if tap < 9:
                spatial_ref[tap, rows, :] = line
            else:
                temporal_ref[tap - 9, rows, :] = line


def assemble(parts):
    return pl.pallas_call(
        assemble_kernel,
        name="assemble",
        out_shape=(
            jax.ShapeDtypeStruct((9, SLICE, CH), F32),
            jax.ShapeDtypeStruct((3, SLICE, CH), F32),
        ),
        in_specs=[VMEM] * CLIPS,
        out_specs=(VMEM, VMEM),
        compiler_params=pltpu.CompilerParams(vmem_limit_bytes=24 << 20),
        cost_estimate=pl.CostEstimate(flops=1000000, bytes_accessed=1200000, transcendentals=0),
    )(*parts)


def send(value, axes, sizes, step):
    n, m = sizes
    pairs = [
        (a * m + b, (a + step[0]) % n * m + (b + step[1]) % m) for a in range(n) for b in range(m)
    ]
    return lax.ppermute(value, axes, pairs)


def around(value, axis, size, step):
    return lax.ppermute(value, axis, [(i, (i + step) % size) for i in range(size)])


def local(sizes, *args):
    return backward(sizes, *args)


def backward(sizes, section_inputs, w_spatial, w_temporal, grad_output, frame_start, frame_count):
    axes = ("pipe", "seq")
    steps = sizes[0]
    x = section_inputs.reshape(CELLS, CH)
    ws, wt = w_spatial[0], w_temporal[0]
    cot = grad_output.reshape(CELLS, CH)
    ahead2 = send(cot, axes, sizes, (0, -2))
    ahead1 = send(cot, axes, sizes, (0, -1))
    mine, slope, wtt, wst, keep = forward(x, wt, ws, frame_start, frame_count)
    head = [keep, cot, ahead1, ahead2]
    head_specs = [VMEM] * 4
    ring = {0: mine}
    half = FRAMES // 2

    def grow(k):
        ring[-k] = around(ring[1 - k], "seq", FRAMES, 2)
        if k < half // 2:
            ring[k] = around(ring[k - 1], "seq", FRAMES, -2)

    grow(1)
    got = []
    for step in range(steps - 1):
        (grad_in,) = small(
            functools.partial(section_kernel, len(got)),
            [(CELLS, CH)],
            head + got + [slope, wtt, wst],
            head_specs + [VMEM] * (len(got) + 3),
            805000000,
            7000000,
        )
        two = send(grad_in, axes, sizes, (-1, -2))
        none = send(grad_in, axes, sizes, (-1, 0))
        (mid,) = small(pick_kernel, [(CELLS, CH)], [two, none], [VMEM] * 2, 0, 400000)
        one = lax.ppermute(mid, "seq", [(i, i ^ 1) for i in range(FRAMES)])
        got = [none, one, two]
        grow(step + 2)
        head[0] = tick(keep)
    late, cot0, grad_pre = small(
        functools.partial(emit_kernel, len(got)),
        [(FRAMES, 2 * SLICE, CELLS), (CELLS, CH), (CELLS, CH)],
        head + got + [slope, wtt],
        head_specs + [VMEM] * (len(got) + 2),
        200000000,
        2000000,
    )
    gathered = lax.all_to_all(late, "seq", 0, 0, tiled=True)
    pieces = [ring[k if k < half // 2 else k - half] for k in range(half)]
    packed = pack(pieces)
    swapped = lax.ppermute(packed, "seq", [(i, i ^ 1) for i in range(FRAMES)])
    (grad_in,) = small(
        spread_kernel, [(CELLS, CH)], [cot0, grad_pre, wst], [VMEM] * 3, 604000000, 5000000
    )
    partial = weights(gathered, pieces, swapped)
    shares = [partial[0]] + [around(partial[k], "dp", CLIPS, k) for k in (1, 2, 3)]
    share = sum(s.astype(F32) for s in shares).astype(BF16)
    share = lax.all_to_all(share, "seq", 0, 0, tiled=True)
    parts = [share] + [around(share, "dp", CLIPS, k) for k in (1, 2, 3)]
    spatial, temporal = assemble(parts)
    return grad_in.reshape(section_inputs.shape), spatial[None], temporal[None]


def solution(mesh):
    sizes = (mesh.shape["pipe"], mesh.shape["seq"])
    placed = (
        P("pipe", "dp", "seq", None, None, None),
        P("pipe", None, None, None),
        P("pipe", None, None, None),
        P("dp", "seq", None, None, None),
        P("dp"),
        P("dp"),
    )
    return jax.shard_map(
        functools.partial(local, sizes),
        mesh=mesh,
        in_specs=placed,
        out_specs=(
            P("pipe", "dp", "seq", None, None, None),
            P("pipe", None, "seq", None),
            P("pipe", None, "seq", None),
        ),
        check_vma=False,
    )
```

```python
import functools

import jax
import jax.numpy as jnp
from jax import lax
from jax.experimental import pallas as pl
from jax.experimental.pallas import tpu as pltpu
from jax.sharding import PartitionSpec as P


F32 = jnp.float32
BF16 = jnp.bfloat16
ANY = pl.BlockSpec(memory_space=pl.ANY)
SMEM = pl.BlockSpec(memory_space=pltpu.SMEM)
VMEM = pl.BlockSpec(memory_space=pltpu.VMEM)
HBM = pl.BlockSpec(memory_space=pltpu.HBM)

ROWS, COLS, CH = 16, 8, 512
CELLS = ROWS * COLS
FRAMES = 16
CLIPS = 4
SLICE = CH // FRAMES
TAPS = 12
WIDE = TAPS * SLICE
SUB = SLICE // CLIPS


def nn(a, b):
    return lax.dot_general(a, b, (((1,), (0,)), ((), ())), preferred_element_type=F32)


def nt(a, b):
    return lax.dot_general(a, b, (((1,), (1,)), ((), ())), preferred_element_type=F32)


def column_shifts(v):
    col = lax.broadcasted_iota(jnp.int32, v.shape, 0) % COLS
    before = jnp.where(col == 0, 0.0, pltpu.roll(v, 1, 0))
    after = jnp.where(col == COLS - 1, 0.0, pltpu.roll(v, CELLS - 1, 0))
    return {0: v, -1: before, 1: after}


def row_shift(v, step):
    zero = jnp.zeros((COLS, v.shape[1]), v.dtype)
    if step == 0:
        return v
    if step < 0:
        return jnp.concatenate([zero, v[:-COLS]], axis=0)
    return jnp.concatenate([v[COLS:], zero], axis=0)


def lead_kernel(zero_ref):
    zero_ref[...] = jnp.zeros((8, CH), F32)


def lead():
    return pl.pallas_call(
        lead_kernel,
        name="lead",
        out_shape=jax.ShapeDtypeStruct((8, CH), F32),
        out_specs=VMEM,
        compiler_params=pltpu.CompilerParams(vmem_limit_bytes=1 << 20),
        cost_estimate=pl.CostEstimate(flops=20000000000, bytes_accessed=16384, transcendentals=0),
    )()


def keep_kernel(start_ref, count_ref, zero_ref, keep_ref):
    seq = lax.axis_index("seq")
    last = lax.axis_index("pipe") == lax.axis_size("pipe") - 1
    t = seq + lax.broadcasted_iota(jnp.int32, (8, CH), 0)
    low = jnp.where(last, start_ref[0], 0)
    high = jnp.where(last, count_ref[0], FRAMES)
    keep_ref[...] = jnp.where((t >= low) & (t < high), 1.0, zero_ref[...])


def keep_of(start, count, zeros):
    return pl.pallas_call(
        keep_kernel,
        name="masks",
        out_shape=jax.ShapeDtypeStruct((8, CH), F32),
        in_specs=[SMEM] * 2 + [VMEM],
        out_specs=VMEM,
        compiler_params=pltpu.CompilerParams(vmem_limit_bytes=1 << 20),
        cost_estimate=pl.CostEstimate(flops=100, bytes_accessed=16384, transcendentals=0),
    )(start, count, zeros)


def forward_kernel(x_ref, wt, ws, cot_hbm, mine_ref, slope_ref, wtt_ref, wst_ref, cot_ref, sem):
    fetch = pltpu.make_async_copy(cot_hbm, cot_ref, sem)
    fetch.start()
    x = x_ref[...].astype(F32)
    cols = column_shifts(x)
    mine_ref[0] = x.T.astype(BF16)
    pre = None
    for r in range(3):
        for q in range(3):
            k = 3 * r + q
            lhs = row_shift(cols[q - 1], r - 1).astype(BF16)
            term = nn(lhs, ws[k])
            pre = term if pre is None else pre + term
            wst_ref[k] = ws[k].T
    s = jax.nn.sigmoid(pre)
    slope_ref[...] = s * (1.0 + pre * (1.0 - s))
    mine_ref[1] = (pre * s).astype(BF16).astype(F32).T.astype(BF16)
    for k in range(3):
        wtt_ref[k] = wt[k].T
    fetch.wait()


def forward(x, wt, ws, cot):
    return pl.pallas_call(
        forward_kernel,
        name="block_forward",
        out_shape=(
            jax.ShapeDtypeStruct((2, CH, CELLS), BF16),
            jax.ShapeDtypeStruct((CELLS, CH), F32),
            jax.ShapeDtypeStruct((3, CH, CH), BF16),
            jax.ShapeDtypeStruct((9, CH, CH), BF16),
            jax.ShapeDtypeStruct((CELLS, CH), BF16),
        ),
        in_specs=[VMEM] * 3 + [HBM],
        out_specs=(VMEM,) * 5,
        scratch_shapes=[pltpu.SemaphoreType.DMA(())],
        compiler_params=pltpu.CompilerParams(vmem_limit_bytes=24 << 20),
        cost_estimate=pl.CostEstimate(flops=1208000000, bytes_accessed=13000000, transcendentals=65536),
    )(x, wt, ws, pltpu.with_memory_space_constraint(cot, pltpu.HBM))


def cotangents(count, refs):
    keep_ref = refs[0]
    own = refs[1:4]
    got = refs[4 : 4 + count]
    last = lax.axis_index("pipe") == lax.axis_size("pipe") - 1
    out = []
    for k in range(3):
        value = own[k][...]
        if count:
            value = jnp.where(last, value, got[k][...])
        keep = keep_ref[k : k + 1, :] != 0.0
        out.append(jnp.where(keep, value.astype(F32), 0.0).astype(BF16))
    return out, refs[4 + count :]


def grad_pre_of(cot, slope_ref, wtt_ref):
    grad_act = nn(cot[0], wtt_ref[0]) + nn(cot[1], wtt_ref[1]) + nn(cot[2], wtt_ref[2])
    return (grad_act.astype(BF16).astype(F32) * slope_ref[...]).astype(BF16)


def spread_of(cot, grad_pre, wst_ref):
    cols = column_shifts(grad_pre.astype(F32))
    total = cot.astype(F32)
    for r in range(3):
        for q in range(3):
            lhs = row_shift(cols[1 - q], 1 - r).astype(BF16)
            total = total + nn(lhs, wst_ref[3 * r + q])
    return total.astype(BF16)


def section_kernel(count, *refs):
    cot, (slope_ref, wtt_ref, wst_ref, gin_ref) = cotangents(count, refs)
    grad_pre = grad_pre_of(cot, slope_ref, wtt_ref)
    gin_ref[...] = spread_of(cot[0], grad_pre, wst_ref)


def emit_kernel(count, *refs):
    cot, (slope_ref, wtt_ref, late_ref, cot_ref, pre_ref) = cotangents(count, refs)
    grad_pre = grad_pre_of(cot, slope_ref, wtt_ref)
    late_ref[:, :SLICE] = grad_pre.astype(F32).T.astype(BF16).reshape(FRAMES, SLICE, CELLS)
    late_ref[:, SLICE:] = cot[0].astype(F32).T.astype(BF16).reshape(FRAMES, SLICE, CELLS)
    cot_ref[...] = cot[0]
    pre_ref[...] = grad_pre


def spread_kernel(cot_ref, pre_ref, wst_ref, gin_ref):
    gin_ref[...] = spread_of(cot_ref[...], pre_ref[...], wst_ref)


def pick_kernel(two_ref, none_ref, out_ref):
    first = lax.axis_index("seq") % 2 == 0
    out_ref[...] = jnp.where(first, two_ref[...], none_ref[...])


def small(kernel, outs, args, specs, flops, read):
    return pl.pallas_call(
        kernel,
        out_shape=tuple(jax.ShapeDtypeStruct(o, BF16) for o in outs),
        in_specs=specs,
        out_specs=(VMEM,) * len(outs),
        compiler_params=pltpu.CompilerParams(vmem_limit_bytes=16 << 20),
        cost_estimate=pl.CostEstimate(flops=flops, bytes_accessed=read, transcendentals=0),
    )(*args)


def pack_kernel(*refs):
    pieces, out, sems = refs[:8], refs[8], refs[9]
    copies = [pltpu.make_async_copy(pieces[k], out.at[k], sems.at[k]) for k in range(8)]
    for c in copies:
        c.start()
    for c in copies:
        c.wait()


def pack(pieces):
    return pl.pallas_call(
        pack_kernel,
        name="pack",
        out_shape=jax.ShapeDtypeStruct((8,) + pieces[0].shape, BF16),
        in_specs=[ANY] * 8,
        out_specs=ANY,
        scratch_shapes=[pltpu.SemaphoreType.DMA((8,))],
        compiler_params=pltpu.CompilerParams(vmem_limit_bytes=4 << 20),
        cost_estimate=pl.CostEstimate(flops=0, bytes_accessed=4000000, transcendentals=0),
    )(*pieces)


def tick_kernel(keep_ref, out_ref):
    out_ref[...] = keep_ref[...]


def tick(keep):
    return pl.pallas_call(
        tick_kernel,
        out_shape=jax.ShapeDtypeStruct(keep.shape, keep.dtype),
        in_specs=[VMEM],
        out_specs=VMEM,
        compiler_params=pltpu.CompilerParams(vmem_limit_bytes=1 << 20),
        cost_estimate=pl.CostEstimate(flops=0, bytes_accessed=32768, transcendentals=0),
    )(keep)


def weights_kernel(late_ref, *refs):
    ring = refs[:8]
    swapped = refs[8]
    outs = refs[9:13]
    left, result = refs[13:]
    seq, d = lax.axis_index("seq"), lax.axis_index("dp")
    z, core = seq // 2, seq % 2
    half = FRAMES // 2
    frame = []
    for k in range(half):
        chip = lax.rem(z + k, half)
        frame += [2 * chip + core, 2 * chip + 1 - core]
    g = jnp.stack([late_ref[t, :SLICE] for t in frame]).astype(F32).reshape(FRAMES * SLICE, CELLS)
    lane = lax.broadcasted_iota(jnp.int32, g.shape, 1)
    row, col = lane // COLS, lane % COLS
    for r in range(3):
        for q in range(3):
            dr, dc = r - 1, q - 1
            v = g if dr == 0 and dc == 0 else pltpu.roll(g, (dr * COLS + dc) % CELLS, 1)
            keep = None
            for at, step, size in ((row, dr, ROWS), (col, dc, COLS)):
                if step:
                    good = (at != 0) if step > 0 else (at != size - 1)
                    keep = good if keep is None else keep & good
            if keep is not None:
                v = jnp.where(keep, v, 0.0)
            v = v.astype(BF16).reshape(FRAMES, SLICE, CELLS)
            base = (3 * r + q) * SLICE
            for f in range(FRAMES):
                left[base : base + SLICE, f * CELLS : (f + 1) * CELLS] = v[f]
    for k in range(3):
        base = (9 + k) * SLICE
        for f in range(FRAMES):
            t = frame[f] + k
            v = late_ref[jnp.minimum(t, FRAMES - 1), SLICE:]
            if k:
                v = jnp.where(t < FRAMES, v, jnp.zeros((SLICE, CELLS), BF16))
            left[base : base + SLICE, f * CELLS : (f + 1) * CELLS] = v
    spatial = temporal = None
    for k in range(half):
        here = slice(2 * k * CELLS, 2 * (k + 1) * CELLS)
        x = jnp.concatenate([ring[k][0], swapped[k, 0]], axis=1)
        act = jnp.concatenate([ring[k][1], swapped[k, 1]], axis=1)
        more = nt(x, left[: 9 * SLICE, here])
        spatial = more if spatial is None else spatial + more
        more = nt(act, left[9 * SLICE :, here])
        temporal = more if temporal is None else temporal + more
    result[:, :, :, : 9 * SLICE] = spatial.reshape(FRAMES, CLIPS, SUB, 9 * SLICE)
    result[:, :, :, 9 * SLICE :] = temporal.reshape(FRAMES, CLIPS, SUB, 3 * SLICE)
    for k in range(CLIPS):
        outs[k][...] = result[:, lax.rem(d + k, CLIPS)].astype(BF16)


def weights(late, ring, swapped):
    return pl.pallas_call(
        weights_kernel,
        name="weight_grads",
        out_shape=(jax.ShapeDtypeStruct((FRAMES, SUB, WIDE), BF16),) * CLIPS,
        in_specs=[VMEM] * 10,
        out_specs=(VMEM,) * CLIPS,
        scratch_shapes=[
            pltpu.VMEM((WIDE, FRAMES * CELLS), BF16),
            pltpu.VMEM((FRAMES, CLIPS, SUB, WIDE), F32),
        ],
        compiler_params=pltpu.CompilerParams(vmem_limit_bytes=24 << 20),
        cost_estimate=pl.CostEstimate(flops=1610000000, bytes_accessed=5000000, transcendentals=0),
    )(late, *ring, swapped)


def assemble_kernel(*refs):
    parts, (spatial_ref, temporal_ref) = refs[:CLIPS], refs[CLIPS:]
    d = lax.axis_index("dp")
    for k in range(CLIPS):
        source = lax.rem(d + CLIPS - k, CLIPS)
        rows = pl.ds(pl.multiple_of(source * SUB, SUB), SUB)
        part = parts[k][...].astype(F32)
        for tap in range(TAPS):
            line = jnp.concatenate(
                [part[s, :, tap * SLICE : (tap + 1) * SLICE] for s in range(FRAMES)], axis=-1
            )
            if tap < 9:
                spatial_ref[tap, rows, :] = line
            else:
                temporal_ref[tap - 9, rows, :] = line


def assemble(parts):
    return pl.pallas_call(
        assemble_kernel,
        name="assemble",
        out_shape=(
            jax.ShapeDtypeStruct((9, SLICE, CH), F32),
            jax.ShapeDtypeStruct((3, SLICE, CH), F32),
        ),
        in_specs=[VMEM] * CLIPS,
        out_specs=(VMEM, VMEM),
        compiler_params=pltpu.CompilerParams(vmem_limit_bytes=24 << 20),
        cost_estimate=pl.CostEstimate(flops=1000000, bytes_accessed=1200000, transcendentals=0),
    )(*parts)


def send(value, axes, sizes, step):
    n, m = sizes
    pairs = [
        (a * m + b, (a + step[0]) % n * m + (b + step[1]) % m) for a in range(n) for b in range(m)
    ]
    return lax.ppermute(value, axes, pairs)


def around(value, axis, size, step):
    return lax.ppermute(value, axis, [(i, (i + step) % size) for i in range(size)])


def local(sizes, *args):
    return backward(sizes, *args)


def backward(sizes, section_inputs, w_spatial, w_temporal, grad_output, frame_start, frame_count):
    axes = ("pipe", "seq")
    steps = sizes[0]
    x = section_inputs.reshape(CELLS, CH)
    ws, wt = w_spatial[0], w_temporal[0]
    cot = grad_output.reshape(CELLS, CH)
    zeros = lead()
    ahead2 = send(cot, axes, sizes, (0, -2))
    ahead1 = send(cot, axes, sizes, (0, -1))
    mine, slope, wtt, wst, cot = forward(x, wt, ws, cot)
    start, count, slope = lax.optimization_barrier((frame_start, frame_count, slope))
    keep = keep_of(start, count, zeros)
    head = [keep, cot, ahead1, ahead2]
    head_specs = [VMEM] * 4
    ring = {0: mine}
    half = FRAMES // 2

    def grow(k):
        ring[-k] = around(ring[1 - k], "seq", FRAMES, 2)
        if k < half // 2:
            ring[k] = around(ring[k - 1], "seq", FRAMES, -2)

    grow(1)
    got = []
    for step in range(steps - 1):
        (grad_in,) = small(
            functools.partial(section_kernel, len(got)),
            [(CELLS, CH)],
            head + got + [slope, wtt, wst],
            head_specs + [VMEM] * (len(got) + 3),
            805000000,
            7000000,
        )
        two = send(grad_in, axes, sizes, (-1, -2))
        none = send(grad_in, axes, sizes, (-1, 0))
        (mid,) = small(pick_kernel, [(CELLS, CH)], [two, none], [VMEM] * 2, 0, 400000)
        one = lax.ppermute(mid, "seq", [(i, i ^ 1) for i in range(FRAMES)])
        got = [none, one, two]
        grow(step + 2)
        head[0] = tick(keep)
    late, cot0, grad_pre = small(
        functools.partial(emit_kernel, len(got)),
        [(FRAMES, 2 * SLICE, CELLS), (CELLS, CH), (CELLS, CH)],
        head + got + [slope, wtt],
        head_specs + [VMEM] * (len(got) + 2),
        200000000,
        2000000,
    )
    gathered = lax.all_to_all(late, "seq", 0, 0, tiled=True)
    pieces = [ring[k if k < half // 2 else k - half] for k in range(half)]
    packed = pack(pieces)
    swapped = lax.ppermute(packed, "seq", [(i, i ^ 1) for i in range(FRAMES)])
    (grad_in,) = small(
        spread_kernel, [(CELLS, CH)], [cot0, grad_pre, wst], [VMEM] * 3, 604000000, 5000000
    )
    partial = weights(gathered, pieces, swapped)
    shares = [partial[0]] + [around(partial[k], "dp", CLIPS, k) for k in (1, 2, 3)]
    share = sum(s.astype(F32) for s in shares).astype(BF16)
    share = lax.all_to_all(share, "seq", 0, 0, tiled=True)
    parts = [share] + [around(share, "dp", CLIPS, k) for k in (1, 2, 3)]
    spatial, temporal = assemble(parts)
    return grad_in.reshape(section_inputs.shape), spatial[None], temporal[None]


def solution(mesh):
    sizes = (mesh.shape["pipe"], mesh.shape["seq"])
    placed = (
        P("pipe", "dp", "seq", None, None, None),
        P("pipe", None, None, None),
        P("pipe", None, None, None),
        P("dp", "seq", None, None, None),
        P("dp"),
        P("dp"),
    )
    return jax.shard_map(
        functools.partial(local, sizes),
        mesh=mesh,
        in_specs=placed,
        out_specs=(
            P("pipe", "dp", "seq", None, None, None),
            P("pipe", None, "seq", None),
            P("pipe", None, "seq", None),
        ),
        check_vma=False,
    )
```

```python
import functools

import jax
import jax.numpy as jnp
from jax import lax
from jax.experimental import pallas as pl
from jax.experimental.pallas import tpu as pltpu
from jax.sharding import PartitionSpec as P


F32 = jnp.float32
BF16 = jnp.bfloat16
ANY = pl.BlockSpec(memory_space=pl.ANY)
SMEM = pl.BlockSpec(memory_space=pltpu.SMEM)
VMEM = pl.BlockSpec(memory_space=pltpu.VMEM)
HBM = pl.BlockSpec(memory_space=pltpu.HBM)

ROWS, COLS, CH = 16, 8, 512
CELLS = ROWS * COLS
FRAMES = 16
CLIPS = 4
SLICE = CH // FRAMES
TAPS = 12
WIDE = TAPS * SLICE
SUB = SLICE // CLIPS


def nn(a, b):
    return lax.dot_general(a, b, (((1,), (0,)), ((), ())), preferred_element_type=F32)


def nt(a, b):
    return lax.dot_general(a, b, (((1,), (1,)), ((), ())), preferred_element_type=F32)


def column_shifts(v):
    col = lax.broadcasted_iota(jnp.int32, v.shape, 0) % COLS
    before = jnp.where(col == 0, 0.0, pltpu.roll(v, 1, 0))
    after = jnp.where(col == COLS - 1, 0.0, pltpu.roll(v, CELLS - 1, 0))
    return {0: v, -1: before, 1: after}


def row_shift(v, step):
    zero = jnp.zeros((COLS, v.shape[1]), v.dtype)
    if step == 0:
        return v
    if step < 0:
        return jnp.concatenate([zero, v[:-COLS]], axis=0)
    return jnp.concatenate([v[COLS:], zero], axis=0)


def lead_kernel(zero_ref):
    zero_ref[...] = jnp.zeros((8, CH), F32)


def lead():
    return pl.pallas_call(
        lead_kernel,
        name="lead",
        out_shape=jax.ShapeDtypeStruct((8, CH), F32),
        out_specs=VMEM,
        compiler_params=pltpu.CompilerParams(vmem_limit_bytes=1 << 20),
        cost_estimate=pl.CostEstimate(flops=20000000000, bytes_accessed=16384, transcendentals=0),
    )()


def keep_kernel(start_ref, count_ref, zero_ref, keep_ref):
    seq = lax.axis_index("seq")
    last = lax.axis_index("pipe") == lax.axis_size("pipe") - 1
    t = seq + lax.broadcasted_iota(jnp.int32, (8, CH), 0)
    low = jnp.where(last, start_ref[0], 0)
    high = jnp.where(last, count_ref[0], FRAMES)
    keep_ref[...] = jnp.where((t >= low) & (t < high), 1.0, zero_ref[...])


def keep_of(start, count, zeros):
    return pl.pallas_call(
        keep_kernel,
        name="masks",
        out_shape=jax.ShapeDtypeStruct((8, CH), F32),
        in_specs=[SMEM] * 2 + [VMEM],
        out_specs=VMEM,
        compiler_params=pltpu.CompilerParams(vmem_limit_bytes=1 << 20),
        cost_estimate=pl.CostEstimate(flops=100, bytes_accessed=16384, transcendentals=0),
    )(start, count, zeros)


def forward_kernel(x_ref, wt, ws, cot_hbm, mine_ref, slope_ref, wtt_ref, wst_ref, cot_ref, sem):
    fetch = pltpu.make_async_copy(cot_hbm, cot_ref, sem)
    fetch.start()
    x = x_ref[...].astype(F32)
    cols = column_shifts(x)
    mine_ref[0] = x.T.astype(BF16)
    pre = None
    for r in range(3):
        for q in range(3):
            k = 3 * r + q
            lhs = row_shift(cols[q - 1], r - 1).astype(BF16)
            term = nn(lhs, ws[k])
            pre = term if pre is None else pre + term
            wst_ref[k] = ws[k].T
    s = jax.nn.sigmoid(pre)
    slope_ref[...] = s * (1.0 + pre * (1.0 - s))
    mine_ref[1] = (pre * s).astype(BF16).astype(F32).T.astype(BF16)
    for k in range(3):
        wtt_ref[k] = wt[k].T
    fetch.wait()


def forward(x, wt, ws, cot):
    return pl.pallas_call(
        forward_kernel,
        name="block_forward",
        out_shape=(
            jax.ShapeDtypeStruct((2, CH, CELLS), BF16),
            jax.ShapeDtypeStruct((CELLS, CH), F32),
            jax.ShapeDtypeStruct((3, CH, CH), BF16),
            jax.ShapeDtypeStruct((9, CH, CH), BF16),
            jax.ShapeDtypeStruct((CELLS, CH), BF16),
        ),
        in_specs=[VMEM] * 3 + [HBM],
        out_specs=(VMEM,) * 5,
        scratch_shapes=[pltpu.SemaphoreType.DMA(())],
        compiler_params=pltpu.CompilerParams(vmem_limit_bytes=24 << 20),
        cost_estimate=pl.CostEstimate(flops=1208000000, bytes_accessed=13000000, transcendentals=65536),
    )(x, wt, ws, pltpu.with_memory_space_constraint(cot, pltpu.HBM))


def cotangents(count, refs):
    keep_ref = refs[0]
    own = refs[1:4]
    got = refs[4 : 4 + count]
    last = lax.axis_index("pipe") == lax.axis_size("pipe") - 1
    out = []
    for k in range(3):
        value = own[k][...]
        if count:
            value = jnp.where(last, value, got[k][...])
        keep = keep_ref[k : k + 1, :] != 0.0
        out.append(jnp.where(keep, value.astype(F32), 0.0).astype(BF16))
    return out, refs[4 + count :]


def grad_pre_of(cot, slope_ref, wtt_ref):
    grad_act = nn(cot[0], wtt_ref[0]) + nn(cot[1], wtt_ref[1]) + nn(cot[2], wtt_ref[2])
    return (grad_act.astype(BF16).astype(F32) * slope_ref[...]).astype(BF16)


def spread_of(cot, grad_pre, wst_ref):
    cols = column_shifts(grad_pre.astype(F32))
    total = cot.astype(F32)
    for r in range(3):
        for q in range(3):
            lhs = row_shift(cols[1 - q], 1 - r).astype(BF16)
            total = total + nn(lhs, wst_ref[3 * r + q])
    return total.astype(BF16)


def section_kernel(count, *refs):
    cot, (slope_ref, wtt_ref, wst_ref, gin_ref) = cotangents(count, refs)
    grad_pre = grad_pre_of(cot, slope_ref, wtt_ref)
    gin_ref[...] = spread_of(cot[0], grad_pre, wst_ref)


def emit_kernel(count, *refs):
    cot, (slope_ref, wtt_ref, late_ref, cot_ref, pre_ref) = cotangents(count, refs)
    grad_pre = grad_pre_of(cot, slope_ref, wtt_ref)
    late_ref[:, :SLICE] = grad_pre.astype(F32).T.astype(BF16).reshape(FRAMES, SLICE, CELLS)
    late_ref[:, SLICE:] = cot[0].astype(F32).T.astype(BF16).reshape(FRAMES, SLICE, CELLS)
    cot_ref[...] = cot[0]
    pre_ref[...] = grad_pre


def spread_kernel(cot_ref, pre_ref, wst_ref, gin_ref):
    gin_ref[...] = spread_of(cot_ref[...], pre_ref[...], wst_ref)


def pick_kernel(two_ref, none_ref, out_ref):
    first = lax.axis_index("seq") % 2 == 0
    out_ref[...] = jnp.where(first, two_ref[...], none_ref[...])


def small(kernel, outs, args, specs, flops, read):
    return pl.pallas_call(
        kernel,
        out_shape=tuple(jax.ShapeDtypeStruct(o, BF16) for o in outs),
        in_specs=specs,
        out_specs=(VMEM,) * len(outs),
        compiler_params=pltpu.CompilerParams(vmem_limit_bytes=16 << 20),
        cost_estimate=pl.CostEstimate(flops=flops, bytes_accessed=read, transcendentals=0),
    )(*args)


def pack_kernel(*refs):
    pieces, out, sems = refs[:8], refs[8], refs[9]
    copies = [pltpu.make_async_copy(pieces[k], out.at[k], sems.at[k]) for k in range(8)]
    for c in copies:
        c.start()
    for c in copies:
        c.wait()


def pack(pieces):
    return pl.pallas_call(
        pack_kernel,
        name="pack",
        out_shape=jax.ShapeDtypeStruct((8,) + pieces[0].shape, BF16),
        in_specs=[ANY] * 8,
        out_specs=ANY,
        scratch_shapes=[pltpu.SemaphoreType.DMA((8,))],
        compiler_params=pltpu.CompilerParams(vmem_limit_bytes=4 << 20),
        cost_estimate=pl.CostEstimate(flops=0, bytes_accessed=4000000, transcendentals=0),
    )(*pieces)


def tick_kernel(keep_ref, out_ref):
    out_ref[...] = keep_ref[...]


def tick(keep):
    return pl.pallas_call(
        tick_kernel,
        out_shape=jax.ShapeDtypeStruct(keep.shape, keep.dtype),
        in_specs=[VMEM],
        out_specs=VMEM,
        compiler_params=pltpu.CompilerParams(vmem_limit_bytes=1 << 20),
        cost_estimate=pl.CostEstimate(flops=0, bytes_accessed=32768, transcendentals=0),
    )(keep)


def weights_kernel(late_ref, *refs):
    ring = refs[:8]
    swapped = refs[8]
    outs = refs[9:13]
    left, result = refs[13:]
    seq, d = lax.axis_index("seq"), lax.axis_index("dp")
    z, core = seq // 2, seq % 2
    half = FRAMES // 2
    frame = []
    for k in range(half):
        chip = lax.rem(z + k, half)
        frame += [2 * chip + core, 2 * chip + 1 - core]
    g = jnp.stack([late_ref[t, :SLICE] for t in frame]).astype(F32).reshape(FRAMES * SLICE, CELLS)
    lane = lax.broadcasted_iota(jnp.int32, g.shape, 1)
    row, col = lane // COLS, lane % COLS
    for r in range(3):
        for q in range(3):
            dr, dc = r - 1, q - 1
            v = g if dr == 0 and dc == 0 else pltpu.roll(g, (dr * COLS + dc) % CELLS, 1)
            keep = None
            for at, step, size in ((row, dr, ROWS), (col, dc, COLS)):
                if step:
                    good = (at != 0) if step > 0 else (at != size - 1)
                    keep = good if keep is None else keep & good
            if keep is not None:
                v = jnp.where(keep, v, 0.0)
            v = v.astype(BF16).reshape(FRAMES, SLICE, CELLS)
            base = (3 * r + q) * SLICE
            for f in range(FRAMES):
                left[base : base + SLICE, f * CELLS : (f + 1) * CELLS] = v[f]
    for k in range(3):
        base = (9 + k) * SLICE
        for f in range(FRAMES):
            t = frame[f] + k
            v = late_ref[jnp.minimum(t, FRAMES - 1), SLICE:]
            if k:
                v = jnp.where(t < FRAMES, v, jnp.zeros((SLICE, CELLS), BF16))
            left[base : base + SLICE, f * CELLS : (f + 1) * CELLS] = v
    spatial = temporal = None
    for k in range(half):
        here = slice(2 * k * CELLS, 2 * (k + 1) * CELLS)
        x = jnp.concatenate([ring[k][0], swapped[k, 0]], axis=1)
        act = jnp.concatenate([ring[k][1], swapped[k, 1]], axis=1)
        more = nt(x, left[: 9 * SLICE, here])
        spatial = more if spatial is None else spatial + more
        more = nt(act, left[9 * SLICE :, here])
        temporal = more if temporal is None else temporal + more
    result[:, :, :, : 9 * SLICE] = spatial.reshape(FRAMES, CLIPS, SUB, 9 * SLICE)
    result[:, :, :, 9 * SLICE :] = temporal.reshape(FRAMES, CLIPS, SUB, 3 * SLICE)
    for k in range(CLIPS):
        outs[k][...] = result[:, lax.rem(d + k, CLIPS)].astype(BF16)


def weights(late, ring, swapped):
    return pl.pallas_call(
        weights_kernel,
        name="weight_grads",
        out_shape=(jax.ShapeDtypeStruct((FRAMES, SUB, WIDE), BF16),) * CLIPS,
        in_specs=[VMEM] * 10,
        out_specs=(VMEM,) * CLIPS,
        scratch_shapes=[
            pltpu.VMEM((WIDE, FRAMES * CELLS), BF16),
            pltpu.VMEM((FRAMES, CLIPS, SUB, WIDE), F32),
        ],
        compiler_params=pltpu.CompilerParams(vmem_limit_bytes=24 << 20),
        cost_estimate=pl.CostEstimate(flops=1610000000, bytes_accessed=5000000, transcendentals=0),
    )(late, *ring, swapped)


def assemble_kernel(sources, kept, *refs):
    parts = refs[: len(sources)]
    spatial_ref, temporal_ref, lines, sems = refs[len(sources) + kept :]
    d = lax.axis_index("dp")
    copies = []
    for i, k in enumerate(sources):
        source = lax.rem(d + CLIPS - k, CLIPS)
        rows = pl.ds(pl.multiple_of(source * SUB, SUB), SUB)
        part = parts[i][...].astype(F32)
        for tap in range(TAPS):
            lines[i, tap] = jnp.concatenate(
                [part[s, :, tap * SLICE : (tap + 1) * SLICE] for s in range(FRAMES)], axis=-1
            )
        for j, (first, size, out) in enumerate(((0, 9, spatial_ref), (9, 3, temporal_ref))):
            c = pltpu.make_async_copy(
                lines.at[i, pl.ds(first, size)], out.at[:, rows, :], sems.at[i, j]
            )
            c.start()
            copies.append(c)
    for c in copies:
        c.wait()


def assemble(sources, parts, outs=()):
    n = len(sources)
    return pl.pallas_call(
        functools.partial(assemble_kernel, sources, len(outs)),
        out_shape=(
            jax.ShapeDtypeStruct((9, SLICE, CH), F32),
            jax.ShapeDtypeStruct((3, SLICE, CH), F32),
        ),
        in_specs=[VMEM] * n + [ANY] * len(outs),
        out_specs=(ANY, ANY),
        scratch_shapes=[
            pltpu.VMEM((n, TAPS, SUB, CH), F32),
            pltpu.SemaphoreType.DMA((n, 2)),
        ],
        input_output_aliases={n + i: i for i in range(len(outs))},
        compiler_params=pltpu.CompilerParams(vmem_limit_bytes=8 << 20),
        cost_estimate=pl.CostEstimate(flops=1000000, bytes_accessed=300000 * n, transcendentals=0),
    )(*parts, *outs)


def send(value, axes, sizes, step):
    n, m = sizes
    pairs = [
        (a * m + b, (a + step[0]) % n * m + (b + step[1]) % m) for a in range(n) for b in range(m)
    ]
    return lax.ppermute(value, axes, pairs)


def around(value, axis, size, step):
    return lax.ppermute(value, axis, [(i, (i + step) % size) for i in range(size)])


def local(sizes, *args):
    return backward(sizes, *args)


def backward(sizes, section_inputs, w_spatial, w_temporal, grad_output, frame_start, frame_count):
    axes = ("pipe", "seq")
    steps = sizes[0]
    x = section_inputs.reshape(CELLS, CH)
    ws, wt = w_spatial[0], w_temporal[0]
    cot = grad_output.reshape(CELLS, CH)
    start, count, zeros = lax.optimization_barrier((frame_start, frame_count, lead()))
    keep = keep_of(start, count, zeros)
    ahead2 = send(cot, axes, sizes, (0, -2))
    ahead1 = send(cot, axes, sizes, (0, -1))
    mine, slope, wtt, wst, cot = forward(x, wt, ws, cot)
    head = [keep, cot, ahead1, ahead2]
    head_specs = [VMEM] * 4
    ring = {0: mine}
    half = FRAMES // 2

    def grow(k):
        ring[-k] = around(ring[1 - k], "seq", FRAMES, 2)
        if k < half // 2:
            ring[k] = around(ring[k - 1], "seq", FRAMES, -2)

    grow(1)
    got = []
    for step in range(steps - 1):
        (grad_in,) = small(
            functools.partial(section_kernel, len(got)),
            [(CELLS, CH)],
            head + got + [slope, wtt, wst],
            head_specs + [VMEM] * (len(got) + 3),
            805000000,
            7000000,
        )
        two = send(grad_in, axes, sizes, (-1, -2))
        none = send(grad_in, axes, sizes, (-1, 0))
        (mid,) = small(pick_kernel, [(CELLS, CH)], [two, none], [VMEM] * 2, 0, 400000)
        one = lax.ppermute(mid, "seq", [(i, i ^ 1) for i in range(FRAMES)])
        got = [none, one, two]
        grow(step + 2)
        head[0] = tick(keep)
    late, cot0, grad_pre = small(
        functools.partial(emit_kernel, len(got)),
        [(FRAMES, 2 * SLICE, CELLS), (CELLS, CH), (CELLS, CH)],
        head + got + [slope, wtt],
        head_specs + [VMEM] * (len(got) + 2),
        200000000,
        2000000,
    )
    gathered = lax.all_to_all(late, "seq", 0, 0, tiled=True)
    pieces = [ring[k if k < half // 2 else k - half] for k in range(half)]
    packed = pack(pieces)
    swapped = lax.ppermute(packed, "seq", [(i, i ^ 1) for i in range(FRAMES)])
    (grad_in,) = small(
        spread_kernel, [(CELLS, CH)], [cot0, grad_pre, wst], [VMEM] * 3, 604000000, 5000000
    )
    partial = weights(gathered, pieces, swapped)
    shares = [partial[0]] + [around(partial[k], "dp", CLIPS, k) for k in (1, 2, 3)]
    share = sum(s.astype(F32) for s in shares).astype(BF16)
    share = lax.all_to_all(share, "seq", 0, 0, tiled=True)
    parts = [share] + [around(share, "dp", CLIPS, k) for k in (1, 2, 3)]
    outs = assemble((0, 3, 2), [parts[k] for k in (0, 3, 2)])
    spatial, temporal = assemble((1,), [parts[1]], outs)
    return grad_in.reshape(section_inputs.shape), spatial[None], temporal[None]


def solution(mesh):
    sizes = (mesh.shape["pipe"], mesh.shape["seq"])
    placed = (
        P("pipe", "dp", "seq", None, None, None),
        P("pipe", None, None, None),
        P("pipe", None, None, None),
        P("dp", "seq", None, None, None),
        P("dp"),
        P("dp"),
    )
    return jax.shard_map(
        functools.partial(local, sizes),
        mesh=mesh,
        in_specs=placed,
        out_specs=(
            P("pipe", "dp", "seq", None, None, None),
            P("pipe", None, "seq", None),
            P("pipe", None, "seq", None),
        ),
        check_vma=False,
    )
```
